32 devices in a mesh: dp: 8 (over y, x, core), tensor: 4 (over z).
Axes of the slice: x: 2, y: 2, z: 4, core: 2. Of those that a mesh axis runs over, the one named last changes fastest.
Arguments:
- inputs: float32 [4096, 768], P(('dp', 'tensor')), may hold values from -6 to 6
- lengths: int32 [8], P('dp'), may hold values from 64 to 512, as said below
- qkv_weight: bfloat16 [1, 3, 768, 768], P(None, None, 'dp', 'tensor'), may hold values from -0.21875 to 0.21875
- qv_bias: float32 [1, 2, 768], P(None, None, 'tensor'), may hold values from -3 to 3
- proj_weight: bfloat16 [1, 768, 768], P(None, 'tensor', 'dp'), may hold values from -1.75 to 1.75
- branch_bias: float32 [1, 2, 768], replicated, may hold values from -3 to 3
- up_weight: bfloat16 [1, 768, 3072], P(None, 'dp', 'tensor'), may hold values from -0.21875 to 0.21875
- up_bias: float32 [1, 3072], P(None, 'tensor'), may hold values from -3 to 3
- down_weight: bfloat16 [1, 3072, 768], P(None, 'tensor', 'dp'), may hold values from -0.109375 to 0.109375
- norm_gain: float32 [1, 2, 768], replicated, may hold values from 0.5 to 1.5
- norm_bias: float32 [1, 2, 768], replicated, may hold values from -3 to 3
- cotangent: float32 [4096, 768], P(('dp', 'tensor')), may hold values from -6 to 6
Outputs:
- outputs: float32 [4096, 768], P(('dp', 'tensor'))
- input_grad: float32 [4096, 768], P(('dp', 'tensor'))
- qkv_grad: float32 [1, 3, 768, 768], P(None, None, 'dp', 'tensor')
- qvbias_grad: float32 [1, 2, 768], P(None, None, 'tensor')
- proj_grad: float32 [1, 768, 768], P(None, 'tensor', 'dp')
- branch_grad: float32 [1, 2, 768], replicated
- up_grad: float32 [1, 768, 3072], P(None, 'dp', 'tensor')
- upbias_grad: float32 [1, 3072], P(None, 'tensor')
- down_grad: float32 [1, 3072, 768], P(None, 'tensor', 'dp')
- gain_grad: float32 [1, 2, 768], replicated
- normbias_grad: float32 [1, 2, 768], replicated
The draws below stay inside these ranges and needn't reach their ends.
Inputs may be any that keep to these rules, and one draw needn't show every extreme that they name: `lengths`: every draw has a sequence with all 512 tokens valid.
All inputs are finite; a program needn't handle non-finite values.
Results may differ from the reference program's by a relative error of at most 0.019.
Values may be sent and summed in bfloat16 or wider, within the bound.
A program may use at most 64 MiB of HBM per device.

```python
import math
import jax
import jax.numpy as jnp
from jax import lax

D = 768
HEADS = 12
HD = 64
FF = 3072
L = 512
LAYERS = 1
SEQS = 8
TOKENS = 4096


def draw_lengths(key, part):
    key_one, key_two = jax.random.split(key)
    drawn = jax.random.randint(key_one, (SEQS,), L // 8, L + 1)
    chosen = jax.random.randint(key_two, (), 0, SEQS)
    return jnp.where(jnp.arange(SEQS) == chosen, L, drawn).astype(jnp.int32)


def raised(values, key, source, target, shards_of, factor):
    def block_of(dim):
        return (jnp.arange(values.shape[dim]) // (values.shape[dim] // shards_of)).reshape((-1,) + (1,) * (values.ndim - 1 - dim))

    near = jax.random.permutation(key, shards_of)[block_of(target)]
    second = (block_of(target) + shards_of // 2) % shards_of
    return jnp.where((block_of(source) == near) | (block_of(source) == second), factor * values, values)


def level_of(rng, extent, cuts, smallest, high):
    def one(dim, blocks):
        draws = jax.random.uniform(jax.random.fold_in(jax.random.fold_in(rng, 6), dim), (blocks,), jnp.float32, smallest / len(cuts), high / len(cuts))
        return jnp.repeat(jnp.exp(draws), extent[dim] // blocks).reshape((-1,) + (1,) * (len(extent) - dim - 1))

    gain = one(*cuts[0])
    for cut in cuts[1:]:
        gain = gain * one(*cut)
    return gain


def noise(own_key, dims, scale, most, pieces=(), kind=jnp.bfloat16):
    values = jax.random.normal(own_key, dims, jnp.float32) * scale
    if len(pieces) > 0:
        values = level_of(own_key, dims, pieces, -0.22, 0.18) * values
    return jnp.clip(values, min=-most, max=most).astype(kind)


def heavy_noise(stream_key, extent, spread, bound, shards, heavy, held_as=jnp.bfloat16):
    result = spread * jax.random.normal(stream_key, extent, jnp.float32)
    if shards:
        result = result * level_of(stream_key, extent, shards, -0.22, 0.18)
    return jnp.clip(raised(result, jax.random.fold_in(stream_key, 3), *heavy), -bound, bound).astype(held_as)


def setup_inputs(seed: int = 0) -> dict:
    splits = jax.random.split(jax.random.key(seed), 13)
    return {
        "inputs": noise(splits[0], (TOKENS, D), 1.0, 6.0, ((0, 32),), jnp.float32),
        "lengths": draw_lengths(jax.random.fold_in(splits[12], 71), 0),
        "qkv_weight": noise(splits[2], (LAYERS, 3, D, D), D ** -0.5, 0.21875, ((2, 8), (3, 4))),
        "qv_bias": noise(splits[3], (LAYERS, 2, D), 0.5, 3.0, ((2, 4),), jnp.float32),
        "proj_weight": noise(splits[4], (LAYERS, D, D), (D // 64) ** -0.5, 1.75, ((1, 4), (2, 8))),
        "branch_bias": noise(splits[5], (LAYERS, 2, D), 0.5, 3.0, (), jnp.float32),
        "up_weight": noise(splits[6], (LAYERS, D, FF), D ** -0.5, 0.21875, ((1, 8), (2, 4))),
        "up_bias": noise(splits[7], (LAYERS, FF), 0.5, 3.0, ((1, 4),), jnp.float32),
        "down_weight": noise(splits[8], (LAYERS, FF, D), FF ** -0.5, 0.109375, ((1, 4), (2, 8))),
        "norm_gain": jnp.clip(1.0 + 0.1 * jax.random.normal(splits[9], (LAYERS, 2, D), jnp.float32), 0.5, 1.5),
        "norm_bias": noise(splits[10], (LAYERS, 2, D), 0.5, 3.0, (), jnp.float32),
        "cotangent": heavy_noise(splits[11], (TOKENS, D), 1.0, 6.0, ((0, 32),), (0, 1, 32, 2.75), jnp.float32),
    }


norm_eps = 1e-12
half_root = 0.7071067811865476
inv_root = 0.3989422804014327

def layer_norm(residual):
    centred = residual - lax.optimization_barrier(jnp.mean(residual, axis=-1, keepdims=True))
    inverse = lax.rsqrt(lax.optimization_barrier(jnp.mean(centred * centred, axis=-1, keepdims=True)) + norm_eps)
    return (centred * inverse, inverse)

def norm_back(upstream, normed, inverse, gain_row):
    scaled = upstream * gain_row
    return inverse * (scaled - lax.optimization_barrier(jnp.mean(scaled, axis=-1, keepdims=True)) - normed * lax.optimization_barrier(jnp.mean(scaled * normed, axis=-1, keepdims=True)))

def gelu_value(pre_act):
    return 0.5 * pre_act * (1.0 + lax.erf(pre_act * half_root))

def gelu_slope(pre_act):
    return 0.5 * (1.0 + lax.erf(pre_act * half_root)) + pre_act * jnp.exp(-0.5 * pre_act * pre_act) * inv_root

def reference(inputs, lengths, qkv_weight, qv_bias, proj_weight, branch_bias, up_weight, up_bias, down_weight, norm_gain, norm_bias, cotangent):
    score_scale = 1.0 / math.sqrt(HD)
    seq_total = lengths.shape[0]
    width = inputs.shape[1]
    positions = jnp.arange(L, dtype=jnp.int32)

    def score_block(queries, key_rows, key_valid):
        raw_scores = jnp.einsum('qhc,khc->hqk', queries.astype(jnp.float32), key_rows.astype(jnp.float32)) * score_scale
        return jnp.where(key_valid[None, None, :], raw_scores, -1e+30)

    def one_sequence(totals, item):
        seq_rows, seq_grad, seq_length = item
        key_valid = positions < seq_length
        stored = []
        hidden = seq_rows
        for layer_index in range(LAYERS):
            rounded = hidden.astype(jnp.bfloat16)
            mixed_rows = jnp.einsum('rd,jde->jre', rounded.astype(jnp.float32), qkv_weight[layer_index].astype(jnp.float32))
            queries = (mixed_rows[0] + qv_bias[layer_index, 0]).astype(jnp.bfloat16).reshape(L, HEADS, HD)
            key_rows = mixed_rows[1].astype(jnp.bfloat16).reshape(L, HEADS, HD)
            values = (mixed_rows[2] + qv_bias[layer_index, 1]).astype(jnp.bfloat16).reshape(L, HEADS, HD)
            scores = score_block(queries, key_rows, key_valid)
            row_peak = lax.optimization_barrier(jnp.max(scores, axis=-1, keepdims=True))
            log_total = row_peak + jnp.log(lax.optimization_barrier(jnp.sum(jnp.exp(scores - row_peak), axis=-1, keepdims=True)))
            soft_weights = jnp.exp(scores - log_total).astype(jnp.bfloat16)
            context = jnp.einsum('hqk,khc->qhc', soft_weights.astype(jnp.float32), values.astype(jnp.float32)).astype(jnp.bfloat16).reshape(L, width)
            residual = hidden + jnp.dot(context, proj_weight[layer_index], preferred_element_type=jnp.float32) + branch_bias[layer_index, 0]
            normed_one, inverse_one = layer_norm(residual)
            middle = normed_one * norm_gain[layer_index, 0] + norm_bias[layer_index, 0]
            middle_rows = middle.astype(jnp.bfloat16)
            pre_act = jnp.dot(middle_rows, up_weight[layer_index], preferred_element_type=jnp.float32) + up_bias[layer_index]
            active = gelu_value(pre_act).astype(jnp.bfloat16)
            residual_two = middle + jnp.dot(active, down_weight[layer_index], preferred_element_type=jnp.float32) + branch_bias[layer_index, 1]
            normed_two, inverse_two = layer_norm(residual_two)
            stored.append((rounded, queries, key_rows, values, log_total, context, normed_one, inverse_one, middle_rows, pre_act, active, normed_two, inverse_two))
            hidden = normed_two * norm_gain[layer_index, 1] + norm_bias[layer_index, 1]
        upstream = seq_grad
        totals = list(totals)
        for layer_index in reversed(range(LAYERS)):
            rounded, queries, key_rows, values, log_total, context, normed_one, inverse_one, middle_rows, pre_act, active, normed_two, inverse_two = stored[layer_index]
            totals[7] = totals[7].at[layer_index, 1].add(lax.optimization_barrier(jnp.sum(upstream * normed_two, axis=0)))
            totals[8] = totals[8].at[layer_index, 1].add(lax.optimization_barrier(jnp.sum(upstream, axis=0)))
            dres_two = norm_back(upstream, normed_two, inverse_two, norm_gain[layer_index, 1])
            totals[3] = totals[3].at[layer_index, 1].add(lax.optimization_barrier(jnp.sum(dres_two, axis=0)))
            dres_two_b = dres_two.astype(jnp.bfloat16)
            totals[6] = totals[6].at[layer_index].add(jnp.dot(active.T, dres_two_b, preferred_element_type=jnp.float32))
            dpre = jnp.dot(dres_two_b, down_weight[layer_index].T, preferred_element_type=jnp.float32) * gelu_slope(pre_act)
            totals[5] = totals[5].at[layer_index].add(lax.optimization_barrier(jnp.sum(dpre, axis=0)))
            dpre_b = dpre.astype(jnp.bfloat16)
            totals[4] = totals[4].at[layer_index].add(jnp.dot(middle_rows.T, dpre_b, preferred_element_type=jnp.float32))
            dmiddle = dres_two + jnp.dot(dpre_b, up_weight[layer_index].T, preferred_element_type=jnp.float32)
            totals[7] = totals[7].at[layer_index, 0].add(lax.optimization_barrier(jnp.sum(dmiddle * normed_one, axis=0)))
            totals[8] = totals[8].at[layer_index, 0].add(lax.optimization_barrier(jnp.sum(dmiddle, axis=0)))
            dres_one = norm_back(dmiddle, normed_one, inverse_one, norm_gain[layer_index, 0])
            totals[3] = totals[3].at[layer_index, 0].add(lax.optimization_barrier(jnp.sum(dres_one, axis=0)))
            dres_one_b = dres_one.astype(jnp.bfloat16)
            totals[2] = totals[2].at[layer_index].add(jnp.dot(context.T, dres_one_b, preferred_element_type=jnp.float32))
            dcontext = jnp.dot(dres_one_b, proj_weight[layer_index].T, preferred_element_type=jnp.float32).astype(jnp.bfloat16).reshape(L, HEADS, HD)
            scores = score_block(queries, key_rows, key_valid)
            probs_full = jnp.exp(scores - log_total)
            dprob = jnp.einsum('qhc,khc->hqk', dcontext.astype(jnp.float32), values.astype(jnp.float32))
            dscore = (probs_full * (dprob - lax.optimization_barrier(jnp.sum(probs_full * dprob, axis=-1, keepdims=True))) * score_scale).astype(jnp.bfloat16)
            dquery = jnp.einsum('hqk,khc->qhc', dscore.astype(jnp.float32), key_rows.astype(jnp.float32))
            dkey = jnp.einsum('hqk,qhc->khc', dscore.astype(jnp.float32), queries.astype(jnp.float32))
            dvalue = jnp.einsum('hqk,qhc->khc', probs_full.astype(jnp.bfloat16).astype(jnp.float32), dcontext.astype(jnp.float32))
            dmixed_full = jnp.stack([dquery, dkey, dvalue]).reshape(3, L, width)
            totals[1] = totals[1].at[layer_index].add(jnp.stack([lax.optimization_barrier(jnp.sum(dmixed_full[0], axis=0)), lax.optimization_barrier(jnp.sum(dmixed_full[2], axis=0))]))
            dmixed = dmixed_full.astype(jnp.bfloat16)
            totals[0] = totals[0].at[layer_index].add(jnp.einsum('rd,jre->jde', rounded.astype(jnp.float32), dmixed.astype(jnp.float32)))
            upstream = dres_one + jnp.einsum('jre,jde->rd', dmixed.astype(jnp.float32), qkv_weight[layer_index].astype(jnp.float32))
        return (tuple(totals), (hidden, upstream))
    zero_totals = (jnp.zeros(qkv_weight.shape, jnp.float32), jnp.zeros(qv_bias.shape, jnp.float32), jnp.zeros(proj_weight.shape, jnp.float32), jnp.zeros(branch_bias.shape, jnp.float32), jnp.zeros(up_weight.shape, jnp.float32), jnp.zeros(up_bias.shape, jnp.float32), jnp.zeros(down_weight.shape, jnp.float32), jnp.zeros(norm_gain.shape, jnp.float32), jnp.zeros(norm_bias.shape, jnp.float32))
    totals, (out_rows, grad_rows) = lax.scan(one_sequence, zero_totals, (inputs.reshape(seq_total, L, width), cotangent.reshape(seq_total, L, width), lengths))
    return (out_rows.reshape(seq_total * L, width), grad_rows.reshape(seq_total * L, width), totals[0], totals[1], totals[2], totals[3], totals[4], totals[5], totals[6], totals[7], totals[8])
```

```python
import functools
import math

import jax
import jax.numpy as jnp
from jax import lax
from jax.experimental import pallas as pl
from jax.experimental.pallas import tpu as pltpu
from jax.sharding import PartitionSpec as P

MESH = pl.DeviceIdType.MESH
BF = jnp.bfloat16
F32 = jnp.float32
HD = 64
L = 512
LAYERS = 1


norm_eps = 1e-12
half_root = 0.7071067811865476
inv_root = 0.3989422804014327


def layer_norm(residual):
    centred = residual - jnp.mean(residual, axis=-1, keepdims=True)
    inverse = lax.rsqrt(jnp.mean(centred * centred, axis=-1, keepdims=True) + norm_eps)
    return (centred * inverse, inverse)


def norm_back(upstream, normed, inverse, gain_row):
    scaled = upstream * gain_row
    return inverse * (
        scaled
        - jnp.mean(scaled, axis=-1, keepdims=True)
        - normed * jnp.mean(scaled * normed, axis=-1, keepdims=True)
    )


def gelu_value(pre_act):
    return 0.5 * pre_act * (1.0 + lax.erf(pre_act * half_root))


def gelu_slope(pre_act):
    return (
        0.5 * (1.0 + lax.erf(pre_act * half_root))
        + pre_act * jnp.exp(-0.5 * pre_act * pre_act) * inv_root
    )


def score_block(queries, key_rows, key_valid):
    raw_scores = jnp.einsum(
        "sqhc,skhc->shqk", queries, key_rows, preferred_element_type=jnp.float32
    ) * (1.0 / math.sqrt(HD))
    return jnp.where(key_valid[:, None, None, :], raw_scores, -1e30)


def send(src, dst, send_sem, recv_sem, axis, target):
    return pltpu.make_async_remote_copy(
        src_ref=src,
        dst_ref=dst,
        send_sem=send_sem,
        recv_sem=recv_sem,
        device_id={axis: target},
        device_id_type=MESH,
    )


def chain_barrier(me, n, extra=0):
    barrier = pltpu.get_barrier_semaphore()

    @pl.when(me > 0)
    def _():
        pl.semaphore_signal(barrier, inc=1, device_id={"tensor": me - 1}, device_id_type=MESH)

    @pl.when(me < n - 1)
    def _():
        pl.semaphore_signal(barrier, inc=1, device_id={"tensor": me + 1}, device_id_type=MESH)

    inner = jnp.logical_and(me > 0, me < n - 1)

    @pl.when(inner)
    def _():
        pl.semaphore_wait(barrier, 2 + extra)

    @pl.when(jnp.logical_not(inner))
    def _():
        pl.semaphore_wait(barrier, 1 + extra)


def ways(me, n):
    return ((0, me, me + 1), (1, n - 1 - me, me - 1))


def chain_reduce(term, me, n, acc, tmp, sbuf, rbuf, ssem, rsem):
    def link(way, s, target):
        return send(
            sbuf.at[way, s], rbuf.at[way, s], ssem.at[way, s], rsem.at[way, s], "tensor", target
        )

    for s in range(n - 1):
        for way, pos, target in ways(me, n):
            owner = n - 1 - s + pos
            block = owner if way == 0 else n - 1 - owner

            @pl.when(pos <= s)
            def _(way=way, pos=pos, target=target, block=block):
                tmp[...] = term(block)
                if s > 0:

                    @pl.when(pos > 0)
                    def _():
                        link(way, s - 1, target).wait_recv()
                        tmp[...] += rbuf[way, s - 1].astype(F32)

                sbuf[way, s] = tmp[...].astype(BF)
                link(way, s, target).start()

    acc[...] = term(me)
    for way, pos, target in ways(me, n):

        @pl.when(pos > 0)
        def _(way=way, target=target):
            link(way, n - 2, target).wait_recv()
            acc[...] += rbuf[way, n - 2].astype(F32)

    def finish():
        for s in range(n - 1):
            for way, pos, target in ways(me, n):

                @pl.when(pos <= s)
                def _(way=way, target=target):
                    link(way, s, target).wait_send()

    return finish


def chain_gather(out, me, n, ssem, rsem, between=None):
    def link(way, s, pos, target):
        block = pos - s
        block = block if way == 0 else n - 1 - block
        return send(
            out.at[block], out.at[block], ssem.at[way, s], rsem.at[way, s], "tensor", target
        )

    for s in range(n - 1):
        for way, pos, target in ways(me, n):

            @pl.when(jnp.logical_and(pos >= s, pos < n - 1))
            def _(way=way, pos=pos, target=target):
                if s > 0:
                    link(way, s - 1, pos - 1, target).wait_recv()
                link(way, s, pos, target).start()

        if s == 0 and between is not None:
            between()
    for way, pos, target in ways(me, n):

        @pl.when(pos == n - 1)
        def _(way=way, pos=pos, target=target):
            for s in range(n - 1):
                link(way, s, pos - 1, target).wait_recv()

    for s in range(n - 1):
        for way, pos, target in ways(me, n):

            @pl.when(jnp.logical_and(pos >= s, pos < n - 1))
            def _(way=way, pos=pos, target=target):
                link(way, s, pos, target).wait_send()


def row_block(ref, block, rows):
    return ref[pl.ds(pl.multiple_of(block * rows, rows), rows), :]


def nt_dot(left, right):
    return lax.dot_general(left, right, (((1,), (1,)), ((), ())), preferred_element_type=F32)


def front_kernel(n, dp, x_ref, qkv_ref, proj_ref, rows_ref, qkv_all, proj_all, gs, gr, ws, wr):
    me = lax.axis_index("tensor")
    mine = lax.axis_index("dp")
    barrier = pltpu.get_barrier_semaphore()
    for k in range(1, dp):
        pl.semaphore_signal(
            barrier, inc=1, device_id={"dp": lax.rem(mine + k, dp)}, device_id_type=MESH
        )
    chain_barrier(me, n, dp - 1)

    def links(k):
        target = lax.rem(mine + k, dp)
        return (
            send(qkv_ref, qkv_all.at[mine], ws.at[0, k], wr.at[0, k], "dp", target),
            send(proj_ref, proj_all.at[mine], ws.at[1, k], wr.at[1, k], "dp", target),
        )

    rows_ref[me] = x_ref[...].astype(BF)

    def between():
        for k in range(1, dp):
            for copy in links(k):
                copy.start()
        qkv_all[mine] = qkv_ref[...]
        proj_all[mine] = proj_ref[...]

    chain_gather(rows_ref, me, n, gs, gr, between)
    for k in range(1, dp):
        for copy in links(k):
            copy.wait()


def attn_out_kernel(
    n, ctx, proj, hidden, bias, gain, nbias,
    normed_o, inv_o, middle_o, rows_o,
    acc, tmp, sbuf, rbuf, ss, sr, gs, gr,
):
    me = lax.axis_index("tensor")
    rows = hidden.shape[0]
    chain_barrier(me, n)
    finish = chain_reduce(
        lambda block: jnp.dot(row_block(ctx, block, rows), proj[...], preferred_element_type=F32),
        me, n, acc, tmp, sbuf, rbuf, ss, sr,
    )
    normed, inverse = layer_norm(hidden[...] + acc[...] + bias[...])
    middle = normed * gain[...] + nbias[...]
    normed_o[...] = normed
    inv_o[...] = inverse
    middle_o[...] = middle
    rows_o[me] = middle.astype(BF)
    chain_gather(rows_o, me, n, gs, gr)
    finish()


def turn_kernel(
    n, act, down, middle, bias, gain, nbias, cot,
    hidden_o, dres_o, sums_o, rows_o,
    acc, tmp, sbuf, rbuf, ss, sr, gs, gr,
):
    me = lax.axis_index("tensor")
    rows = middle.shape[0]
    chain_barrier(me, n)
    finish = chain_reduce(
        lambda block: jnp.dot(row_block(act, block, rows), down[...], preferred_element_type=F32),
        me, n, acc, tmp, sbuf, rbuf, ss, sr,
    )
    normed, inverse = layer_norm(middle[...] + acc[...] + bias[...])
    acc[...] = normed
    dres = norm_back(cot[...], normed, inverse, gain[...])
    dres_o[...] = dres
    rows_o[me] = dres.astype(BF)

    def between():
        hidden_o[...] = acc[...] * gain[...] + nbias[...]
        sums_o[0:1, :] = jnp.sum(cot[...] * acc[...], axis=0, keepdims=True)
        sums_o[1:2, :] = jnp.sum(cot[...], axis=0, keepdims=True)
        sums_o[2:3, :] = jnp.sum(dres_o[...], axis=0, keepdims=True)

    chain_gather(rows_o, me, n, gs, gr, between)
    finish()


def mid_back_kernel(
    n, dpre, up, dres_two, normed, inverse, gain,
    dres_o, sums_o, rows_o,
    acc, tmp, sbuf, rbuf, ss, sr, gs, gr,
):
    me = lax.axis_index("tensor")
    rows = normed.shape[0]
    chain_barrier(me, n)
    finish = chain_reduce(
        lambda block: nt_dot(row_block(dpre, block, rows), up[...]),
        me, n, acc, tmp, sbuf, rbuf, ss, sr,
    )
    acc[...] += dres_two[...]
    dres = norm_back(acc[...], normed[...], inverse[...], gain[...])
    dres_o[...] = dres
    rows_o[me] = dres.astype(BF)

    def between():
        sums_o[0:1, :] = jnp.sum(acc[...] * normed[...], axis=0, keepdims=True)
        sums_o[1:2, :] = jnp.sum(acc[...], axis=0, keepdims=True)
        sums_o[2:3, :] = jnp.sum(dres_o[...], axis=0, keepdims=True)

    chain_gather(rows_o, me, n, gs, gr, between)
    finish()


def last_kernel(n, dmix, qkv, dres, up_o, acc, tmp, sbuf, rbuf, ss, sr):
    me = lax.axis_index("tensor")
    rows = dres.shape[0]
    chain_barrier(me, n)

    def term(block):
        return sum(nt_dot(row_block(dmix.at[j], block, rows), qkv[j]) for j in range(3))

    finish = chain_reduce(term, me, n, acc, tmp, sbuf, rbuf, ss, sr)
    up_o[...] = dres[...] + acc[...]
    finish()


def run(body, number, outs, scratch, flops, *operands):
    vmem = pl.BlockSpec(memory_space=pltpu.VMEM)
    return pl.pallas_call(
        body,
        out_shape=[jax.ShapeDtypeStruct(shape, dtype) for shape, dtype in outs],
        in_specs=[vmem] * len(operands),
        out_specs=[vmem] * len(outs),
        scratch_shapes=scratch,
        cost_estimate=pl.CostEstimate(flops=flops, bytes_accessed=60_000_000, transcendentals=0),
        compiler_params=pltpu.CompilerParams(
            collective_id=number, has_side_effects=True, vmem_limit_bytes=40 * 2**20
        ),
    )(*operands)


def reduce_scratch(n, rows, width):
    return [
        pltpu.VMEM((rows, width), F32),
        pltpu.VMEM((rows, width), F32),
        pltpu.VMEM((2, n - 1, rows, width), BF),
        pltpu.VMEM((2, n - 1, rows, width), BF),
    ] + chain_sems(n)


def chain_sems(n):
    return [pltpu.SemaphoreType.DMA((2, n - 1)), pltpu.SemaphoreType.DMA((2, n - 1))]


def per_device(
    inputs,
    lengths,
    qkv_weight,
    qv_bias,
    proj_weight,
    branch_bias,
    up_weight,
    up_bias,
    down_weight,
    norm_gain,
    norm_bias,
    cotangent,
):
    n = lax.axis_size("tensor")
    dp = lax.axis_size("dp")
    own_rows, width = inputs.shape
    seq_count = lengths.shape[0]
    local = qkv_weight.shape[3]
    head_count = local // HD
    head_shape = (seq_count, L, head_count, HD)
    key_valid = jnp.arange(L, dtype=jnp.int32)[None, :] < lengths[:, None]
    total_rows = own_rows * n
    own = (own_rows, width)
    spread = ((n, own_rows, width), BF)
    sums = ((3, width), F32)
    up_full = lax.all_gather(up_weight[0], "dp", axis=0, tiled=True)
    down_full = lax.all_gather(down_weight[0], "dp", axis=1, tiled=True)
    rounded, qkv_blocks, proj_blocks = run(
        functools.partial(front_kernel, n, dp),
        0,
        [spread, ((dp,) + qkv_weight.shape[1:], BF), ((dp,) + proj_weight.shape[1:], BF)],
        chain_sems(n)
        + [pltpu.SemaphoreType.DMA((2, dp)), pltpu.SemaphoreType.DMA((2, dp))],
        0,
        inputs,
        qkv_weight[0],
        proj_weight[0],
    )
    rounded = rounded.reshape(total_rows, width)
    qkv_full = qkv_blocks.transpose(1, 0, 2, 3).reshape(3, width, local)
    proj_full = proj_blocks.transpose(1, 0, 2).reshape(local, width)
    mixed_rows = jnp.einsum("rd,jde->jre", rounded, qkv_full, preferred_element_type=F32)
    queries = (mixed_rows[0] + qv_bias[0, 0]).astype(BF).reshape(head_shape)
    key_rows = mixed_rows[1].astype(BF).reshape(head_shape)
    values = (mixed_rows[2] + qv_bias[0, 1]).astype(BF).reshape(head_shape)
    scores = score_block(queries, key_rows, key_valid)
    row_peak = jnp.max(scores, axis=-1, keepdims=True)
    log_total = row_peak + jnp.log(jnp.sum(jnp.exp(scores - row_peak), axis=-1, keepdims=True))
    soft_weights = jnp.exp(scores - log_total).astype(BF)
    context = (
        jnp.einsum("shqk,skhc->sqhc", soft_weights, values, preferred_element_type=F32)
        .astype(BF)
        .reshape(total_rows, local)
    )
    normed_one, inverse_one, middle, middle_rows = run(
        functools.partial(attn_out_kernel, n),
        1,
        [(own, F32), ((own_rows, 1), F32), (own, F32), spread],
        reduce_scratch(n, own_rows, width) + chain_sems(n),
        2 * total_rows * local * width,
        context,
        proj_full,
        inputs,
        branch_bias[0, 0:1],
        norm_gain[0, 0:1],
        norm_bias[0, 0:1],
    )
    middle_rows = middle_rows.reshape(total_rows, width)
    pre_act = jnp.dot(middle_rows, up_full, preferred_element_type=F32) + up_bias[0]
    active = gelu_value(pre_act).astype(BF)
    hidden, dres_two, sums_two, dres_two_all = run(
        functools.partial(turn_kernel, n),
        2,
        [(own, F32), (own, F32), sums, spread],
        reduce_scratch(n, own_rows, width) + chain_sems(n),
        2 * total_rows * width * active.shape[1],
        active,
        down_full,
        middle,
        branch_bias[0, 1:2],
        norm_gain[0, 1:2],
        norm_bias[0, 1:2],
        cotangent,
    )
    dres_two_all = dres_two_all.reshape(total_rows, width)
    dpre = jnp.einsum(
        "rd,fd->rf", dres_two_all, down_full, preferred_element_type=F32
    ) * gelu_slope(pre_act)
    upbias_part = jnp.sum(dpre, axis=0)
    dpre_b = dpre.astype(BF)
    down_part = jnp.einsum("rf,rd->fd", active, dres_two_all, preferred_element_type=F32)
    up_part = jnp.einsum("rd,rf->df", middle_rows, dpre_b, preferred_element_type=F32)
    up_out = lax.psum_scatter(up_part.astype(BF), "dp", scatter_dimension=0, tiled=True)
    down_out = lax.psum_scatter(down_part.astype(BF), "dp", scatter_dimension=1, tiled=True)
    dres_one, sums_one, dres_one_all = run(
        functools.partial(mid_back_kernel, n),
        3,
        [(own, F32), sums, spread],
        reduce_scratch(n, own_rows, width) + chain_sems(n),
        2 * total_rows * width * dpre_b.shape[1],
        dpre_b,
        up_full,
        dres_two,
        normed_one,
        inverse_one,
        norm_gain[0, 0:1],
    )
    dres_one_all = dres_one_all.reshape(total_rows, width)
    proj_part = jnp.einsum("rc,rd->cd", context, dres_one_all, preferred_element_type=F32)
    dcontext = (
        jnp.einsum("rd,cd->rc", dres_one_all, proj_full, preferred_element_type=F32)
        .astype(BF)
        .reshape(head_shape)
    )
    scores = score_block(queries, key_rows, key_valid)
    probs_full = jnp.exp(scores - log_total)
    dprob = jnp.einsum("sqhc,skhc->shqk", dcontext, values, preferred_element_type=F32)
    dscore = (
        probs_full
        * (dprob - jnp.sum(probs_full * dprob, axis=-1, keepdims=True))
        * (1.0 / math.sqrt(HD))
    ).astype(BF)
    dquery = jnp.einsum("shqk,skhc->sqhc", dscore, key_rows, preferred_element_type=F32)
    dkey = jnp.einsum("shqk,sqhc->skhc", dscore, queries, preferred_element_type=F32)
    dvalue = jnp.einsum("shqk,sqhc->skhc", probs_full.astype(BF), dcontext, preferred_element_type=F32)
    dmixed_full = jnp.stack([dquery, dkey, dvalue]).reshape(3, total_rows, local)
    qvbias_part = jnp.stack([jnp.sum(dmixed_full[0], axis=0), jnp.sum(dmixed_full[2], axis=0)])
    dmixed = dmixed_full.astype(BF)
    qkv_part = jnp.einsum("rd,jre->jde", rounded, dmixed, preferred_element_type=F32)
    upstream = run(
        functools.partial(last_kernel, n),
        4,
        [(own, F32)],
        reduce_scratch(n, own_rows, width),
        6 * total_rows * local * width,
        dmixed,
        qkv_full,
        dres_one,
    )[0]
    qkv_out = lax.psum_scatter(qkv_part.astype(BF), "dp", scatter_dimension=1, tiled=True)
    proj_out = lax.psum_scatter(proj_part.astype(BF), "dp", scatter_dimension=1, tiled=True)
    qvbias_out, upbias_out = lax.psum((qvbias_part, upbias_part), "dp")
    all_sums = lax.psum(jnp.stack([sums_one, sums_two], axis=1), ("dp", "tensor"))
    gain_out, normbias_out, branch_out = all_sums[0], all_sums[1], all_sums[2]
    return (
        hidden,
        upstream,
        qkv_out.astype(F32)[None],
        qvbias_out[None],
        proj_out.astype(F32)[None],
        branch_out[None],
        up_out.astype(F32)[None],
        upbias_out[None],
        down_out.astype(F32)[None],
        gain_out[None],
        normbias_out[None],
    )


def solution(mesh):
    placed = (
        P(("dp", "tensor"), None),
        P("dp"),
        P(None, None, "dp", "tensor"),
        P(None, None, "tensor"),
        P(None, "tensor", "dp"),
        P(),
        P(None, "dp", "tensor"),
        P(None, "tensor"),
        P(None, "tensor", "dp"),
        P(),
        P(),
        P(("dp", "tensor"), None),
    )
    return jax.shard_map(
        per_device,
        mesh=mesh,
        in_specs=placed,
        out_specs=(
            P(("dp", "tensor"), None),
            P(("dp", "tensor"), None),
            P(None, None, "dp", "tensor"),
            P(None, None, "tensor"),
            P(None, "tensor", "dp"),
            P(),
            P(None, "dp", "tensor"),
            P(None, "tensor"),
            P(None, "tensor", "dp"),
            P(),
            P(),
        ),
        check_vma=False,
    )
```

```python
import functools
import math

import jax
import jax.numpy as jnp
from jax import lax
from jax.experimental import pallas as pl
from jax.experimental.pallas import tpu as pltpu
from jax.sharding import PartitionSpec as P

MESH = pl.DeviceIdType.MESH
BF = jnp.bfloat16
F32 = jnp.float32
HD = 64
L = 512
LAYERS = 1


norm_eps = 1e-12
half_root = 0.7071067811865476
inv_root = 0.3989422804014327


def layer_norm(residual):
    centred = residual - jnp.mean(residual, axis=-1, keepdims=True)
    inverse = lax.rsqrt(jnp.mean(centred * centred, axis=-1, keepdims=True) + norm_eps)
    return (centred * inverse, inverse)


def norm_back(upstream, normed, inverse, gain_row):
    scaled = upstream * gain_row
    return inverse * (
        scaled
        - jnp.mean(scaled, axis=-1, keepdims=True)
        - normed * jnp.mean(scaled * normed, axis=-1, keepdims=True)
    )


def gelu_value(pre_act):
    return 0.5 * pre_act * (1.0 + lax.erf(pre_act * half_root))


def gelu_slope(pre_act):
    return (
        0.5 * (1.0 + lax.erf(pre_act * half_root))
        + pre_act * jnp.exp(-0.5 * pre_act * pre_act) * inv_root
    )


def score_block(queries, key_rows, key_valid):
    raw_scores = jnp.einsum(
        "sqhc,skhc->shqk", queries, key_rows, preferred_element_type=jnp.float32
    ) * (1.0 / math.sqrt(HD))
    return jnp.where(key_valid[:, None, None, :], raw_scores, -1e30)


def send(src, dst, send_sem, recv_sem, axis, target):
    return pltpu.make_async_remote_copy(
        src_ref=src,
        dst_ref=dst,
        send_sem=send_sem,
        recv_sem=recv_sem,
        device_id={axis: target},
        device_id_type=MESH,
    )


def chain_barrier(me, n, extra=0):
    barrier = pltpu.get_barrier_semaphore()

    @pl.when(me > 0)
    def _():
        pl.semaphore_signal(barrier, inc=1, device_id={"tensor": me - 1}, device_id_type=MESH)

    @pl.when(me < n - 1)
    def _():
        pl.semaphore_signal(barrier, inc=1, device_id={"tensor": me + 1}, device_id_type=MESH)

    inner = jnp.logical_and(me > 0, me < n - 1)

    @pl.when(inner)
    def _():
        pl.semaphore_wait(barrier, 2 + extra)

    @pl.when(jnp.logical_not(inner))
    def _():
        pl.semaphore_wait(barrier, 1 + extra)


def group_signal(axis, size):
    mine = lax.axis_index(axis)
    for k in range(1, size):
        pl.semaphore_signal(
            pltpu.get_barrier_semaphore(),
            inc=1,
            device_id={axis: lax.rem(mine + k, size)},
            device_id_type=MESH,
        )


def owners_copy(part, got, ssem, rsem, slot, dp, k):
    target = lax.rem(lax.axis_index("dp") + k, dp)
    return send(part.at[target], got.at[k], ssem.at[slot, k], rsem.at[slot, k], "dp", target)


def owners_sum(parts, gots, outs, ssem, rsem, dp):
    mine = lax.axis_index("dp")
    for slot, (part, got, out) in enumerate(zip(parts, gots, outs)):
        out[...] = part[mine].astype(F32)
        for k in range(1, dp):
            owners_copy(part, got, ssem, rsem, slot, dp, k).wait()
            out[...] += got[k].astype(F32)


def share_copy(got, ssem, rsem, slot, axis, size, k):
    mine = lax.axis_index(axis)
    target = lax.rem(mine + k, size)
    return send(got.at[mine], got.at[mine], ssem.at[slot, k], rsem.at[slot, k], axis, target)


def share_sum(got, ssem, rsem, slot, axis, size):
    for k in range(1, size):
        share_copy(got, ssem, rsem, slot, axis, size, k).wait()
    total = got[0]
    for k in range(1, size):
        total = total + got[k]
    return total


def ways(me, n):
    return ((0, me, me + 1), (1, n - 1 - me, me - 1))


def chain_reduce(term, me, n, acc, tmp, sbuf, rbuf, ssem, rsem):
    def link(way, s, target):
        return send(
            sbuf.at[way, s], rbuf.at[way, s], ssem.at[way, s], rsem.at[way, s], "tensor", target
        )

    for s in range(n - 1):
        for way, pos, target in ways(me, n):
            owner = n - 1 - s + pos
            block = owner if way == 0 else n - 1 - owner

            @pl.when(pos <= s)
            def _(way=way, pos=pos, target=target, block=block):
                tmp[...] = term(block)
                if s > 0:

                    @pl.when(pos > 0)
                    def _():
                        link(way, s - 1, target).wait_recv()
                        tmp[...] += rbuf[way, s - 1].astype(F32)

                sbuf[way, s] = tmp[...].astype(BF)
                link(way, s, target).start()

    acc[...] = term(me)
    for way, pos, target in ways(me, n):

        @pl.when(pos > 0)
        def _(way=way, target=target):
            link(way, n - 2, target).wait_recv()
            acc[...] += rbuf[way, n - 2].astype(F32)

    def finish():
        for s in range(n - 1):
            for way, pos, target in ways(me, n):

                @pl.when(pos <= s)
                def _(way=way, target=target):
                    link(way, s, target).wait_send()

    return finish


def chain_gather(out, me, n, ssem, rsem, between=None):
    def link(way, s, pos, target):
        block = pos - s
        block = block if way == 0 else n - 1 - block
        return send(
            out.at[block], out.at[block], ssem.at[way, s], rsem.at[way, s], "tensor", target
        )

    for s in range(n - 1):
        for way, pos, target in ways(me, n):

            @pl.when(jnp.logical_and(pos >= s, pos < n - 1))
            def _(way=way, pos=pos, target=target):
                if s > 0:
                    link(way, s - 1, pos - 1, target).wait_recv()
                link(way, s, pos, target).start()

        if s == 0 and between is not None:
            between()
    for way, pos, target in ways(me, n):

        @pl.when(pos == n - 1)
        def _(way=way, pos=pos, target=target):
            for s in range(n - 1):
                link(way, s, pos - 1, target).wait_recv()

    for s in range(n - 1):
        for way, pos, target in ways(me, n):

            @pl.when(jnp.logical_and(pos >= s, pos < n - 1))
            def _(way=way, pos=pos, target=target):
                link(way, s, pos, target).wait_send()


def row_block(ref, block, rows):
    return ref[pl.ds(pl.multiple_of(block * rows, rows), rows), :]


def nt_dot(left, right):
    return lax.dot_general(left, right, (((1,), (1,)), ((), ())), preferred_element_type=F32)


def front_kernel(n, dp, x_ref, qkv_ref, proj_ref, rows_ref, qkv_all, proj_all, gs, gr, ws, wr):
    me = lax.axis_index("tensor")
    mine = lax.axis_index("dp")
    barrier = pltpu.get_barrier_semaphore()
    for k in range(1, dp):
        pl.semaphore_signal(
            barrier, inc=1, device_id={"dp": lax.rem(mine + k, dp)}, device_id_type=MESH
        )
    chain_barrier(me, n, dp - 1)

    def links(k):
        target = lax.rem(mine + k, dp)
        return (
            send(qkv_ref, qkv_all.at[mine], ws.at[0, k], wr.at[0, k], "dp", target),
            send(proj_ref, proj_all.at[mine], ws.at[1, k], wr.at[1, k], "dp", target),
        )

    rows_ref[me] = x_ref[...].astype(BF)

    def between():
        for k in range(1, dp):
            for copy in links(k):
                copy.start()
        qkv_all[mine] = qkv_ref[...]
        proj_all[mine] = proj_ref[...]

    chain_gather(rows_ref, me, n, gs, gr, between)
    for k in range(1, dp):
        for copy in links(k):
            copy.wait()


def attn_out_kernel(
    n, ctx, proj, hidden, bias, gain, nbias,
    normed_o, inv_o, middle_o, rows_o,
    acc, tmp, sbuf, rbuf, ss, sr, gs, gr,
):
    me = lax.axis_index("tensor")
    rows = hidden.shape[0]
    chain_barrier(me, n)
    finish = chain_reduce(
        lambda block: jnp.dot(row_block(ctx, block, rows), proj[...], preferred_element_type=F32),
        me, n, acc, tmp, sbuf, rbuf, ss, sr,
    )
    normed, inverse = layer_norm(hidden[...] + acc[...] + bias[...])
    middle = normed * gain[...] + nbias[...]
    normed_o[...] = normed
    inv_o[...] = inverse
    middle_o[...] = middle
    rows_o[me] = middle.astype(BF)
    chain_gather(rows_o, me, n, gs, gr)
    finish()


def turn_kernel(
    n, act, down, middle, bias, gain, nbias, cot,
    hidden_o, dres_o, sums_o, rows_o,
    acc, tmp, sbuf, rbuf, ss, sr, gs, gr,
):
    me = lax.axis_index("tensor")
    rows = middle.shape[0]
    chain_barrier(me, n)
    finish = chain_reduce(
        lambda block: jnp.dot(row_block(act, block, rows), down[...], preferred_element_type=F32),
        me, n, acc, tmp, sbuf, rbuf, ss, sr,
    )
    normed, inverse = layer_norm(middle[...] + acc[...] + bias[...])
    acc[...] = normed
    dres = norm_back(cot[...], normed, inverse, gain[...])
    dres_o[...] = dres
    rows_o[me] = dres.astype(BF)

    def between():
        hidden_o[...] = acc[...] * gain[...] + nbias[...]
        sums_o[0:1, :] = jnp.sum(cot[...] * acc[...], axis=0, keepdims=True)
        sums_o[1:2, :] = jnp.sum(cot[...], axis=0, keepdims=True)
        sums_o[2:3, :] = jnp.sum(dres_o[...], axis=0, keepdims=True)

    chain_gather(rows_o, me, n, gs, gr, between)
    finish()


def mid_back_kernel(
    n, dp, dpre, up, dres_two, normed, inverse, gain, up_part, down_part,
    dres_o, sums_o, rows_o, up_o, down_o,
    acc, tmp, sbuf, rbuf, ss, sr, gs, gr, up_got, down_got, ws, wr,
):
    me = lax.axis_index("tensor")
    rows = normed.shape[0]
    group_signal("dp", dp)
    chain_barrier(me, n, dp - 1)
    parts, gots, outs = (up_part, down_part), (up_got, down_got), (up_o, down_o)
    for k in range(1, dp):
        for slot in range(2):
            owners_copy(parts[slot], gots[slot], ws, wr, slot, dp, k).start()
    finish = chain_reduce(
        lambda block: nt_dot(row_block(dpre, block, rows), up[...]),
        me, n, acc, tmp, sbuf, rbuf, ss, sr,
    )
    acc[...] += dres_two[...]
    dres = norm_back(acc[...], normed[...], inverse[...], gain[...])
    dres_o[...] = dres
    rows_o[me] = dres.astype(BF)

    def between():
        sums_o[0:1, :] = jnp.sum(acc[...] * normed[...], axis=0, keepdims=True)
        sums_o[1:2, :] = jnp.sum(acc[...], axis=0, keepdims=True)
        sums_o[2:3, :] = jnp.sum(dres_o[...], axis=0, keepdims=True)

    chain_gather(rows_o, me, n, gs, gr, between)
    finish()
    owners_sum(parts, gots, outs, ws, wr, dp)


def last_kernel(
    n, dp, dmix, qkv, dres, qkv_part, proj_part, sums, biases,
    up_o, qkv_o, proj_o, sums_o, biases_o,
    acc, tmp, sbuf, rbuf, ss, sr, qkv_got, proj_got, ws, wr, sums_got, biases_got, sums_all, ts, tr,
):
    me = lax.axis_index("tensor")
    mine = lax.axis_index("dp")
    rows = dres.shape[0]
    group_signal("dp", dp)
    group_signal("tensor", n)
    pl.semaphore_wait(pltpu.get_barrier_semaphore(), dp + n - 2)
    sums_got[mine] = sums[...]
    biases_got[mine] = biases[...]
    parts, gots, outs = (qkv_part, proj_part), (qkv_got, proj_got), (qkv_o, proj_o)
    for k in range(1, dp):
        share_copy(sums_got, ws, wr, 2, "dp", dp, k).start()
        share_copy(biases_got, ws, wr, 3, "dp", dp, k).start()
    for k in range(1, dp):
        for slot in range(2):
            owners_copy(parts[slot], gots[slot], ws, wr, slot, dp, k).start()

    def term(block):
        return sum(nt_dot(row_block(dmix.at[j], block, rows), qkv[j]) for j in range(3))

    finish = chain_reduce(term, me, n, acc, tmp, sbuf, rbuf, ss, sr)
    sums_all[me] = share_sum(sums_got, ws, wr, 2, "dp", dp)
    for k in range(1, n):
        share_copy(sums_all, ts, tr, 0, "tensor", n, k).start()
    biases_o[...] = share_sum(biases_got, ws, wr, 3, "dp", dp)
    up_o[...] = dres[...] + acc[...]
    owners_sum(parts, gots, outs, ws, wr, dp)
    finish()
    sums_o[...] = share_sum(sums_all, ts, tr, 0, "tensor", n)


def run(body, number, outs, scratch, flops, *operands):
    vmem = pl.BlockSpec(memory_space=pltpu.VMEM)
    return pl.pallas_call(
        body,
        out_shape=[jax.ShapeDtypeStruct(shape, dtype) for shape, dtype in outs],
        in_specs=[vmem] * len(operands),
        out_specs=[vmem] * len(outs),
        scratch_shapes=scratch,
        cost_estimate=pl.CostEstimate(flops=flops, bytes_accessed=60_000_000, transcendentals=0),
        compiler_params=pltpu.CompilerParams(
            collective_id=number, has_side_effects=True, vmem_limit_bytes=40 * 2**20
        ),
    )(*operands)


def reduce_scratch(n, rows, width):
    return [
        pltpu.VMEM((rows, width), F32),
        pltpu.VMEM((rows, width), F32),
        pltpu.VMEM((2, n - 1, rows, width), BF),
        pltpu.VMEM((2, n - 1, rows, width), BF),
    ] + chain_sems(n)


def chain_sems(n):
    return [pltpu.SemaphoreType.DMA((2, n - 1)), pltpu.SemaphoreType.DMA((2, n - 1))]


def per_device(
    inputs,
    lengths,
    qkv_weight,
    qv_bias,
    proj_weight,
    branch_bias,
    up_weight,
    up_bias,
    down_weight,
    norm_gain,
    norm_bias,
    cotangent,
):
    n = lax.axis_size("tensor")
    dp = lax.axis_size("dp")
    own_rows, width = inputs.shape
    seq_count = lengths.shape[0]
    local = qkv_weight.shape[3]
    head_count = local // HD
    head_shape = (seq_count, L, head_count, HD)
    key_valid = jnp.arange(L, dtype=jnp.int32)[None, :] < lengths[:, None]
    total_rows = own_rows * n
    own = (own_rows, width)
    spread = ((n, own_rows, width), BF)
    sums = ((3, width), F32)
    up_full = lax.all_gather(up_weight[0], "dp", axis=0, tiled=True)
    down_full = lax.all_gather(down_weight[0], "dp", axis=1, tiled=True)
    rounded, qkv_blocks, proj_blocks = run(
        functools.partial(front_kernel, n, dp),
        0,
        [spread, ((dp,) + qkv_weight.shape[1:], BF), ((dp,) + proj_weight.shape[1:], BF)],
        chain_sems(n)
        + [pltpu.SemaphoreType.DMA((2, dp)), pltpu.SemaphoreType.DMA((2, dp))],
        0,
        inputs,
        qkv_weight[0],
        proj_weight[0],
    )
    rounded = rounded.reshape(total_rows, width)
    qkv_full = qkv_blocks.transpose(1, 0, 2, 3).reshape(3, width, local)
    proj_full = proj_blocks.transpose(1, 0, 2).reshape(local, width)
    mixed_rows = jnp.einsum("rd,jde->jre", rounded, qkv_full, preferred_element_type=F32)
    queries = (mixed_rows[0] + qv_bias[0, 0]).astype(BF).reshape(head_shape)
    key_rows = mixed_rows[1].astype(BF).reshape(head_shape)
    values = (mixed_rows[2] + qv_bias[0, 1]).astype(BF).reshape(head_shape)
    scores = score_block(queries, key_rows, key_valid)
    row_peak = jnp.max(scores, axis=-1, keepdims=True)
    log_total = row_peak + jnp.log(jnp.sum(jnp.exp(scores - row_peak), axis=-1, keepdims=True))
    soft_weights = jnp.exp(scores - log_total).astype(BF)
    context = (
        jnp.einsum("shqk,skhc->sqhc", soft_weights, values, preferred_element_type=F32)
        .astype(BF)
        .reshape(total_rows, local)
    )
    normed_one, inverse_one, middle, middle_rows = run(
        functools.partial(attn_out_kernel, n),
        1,
        [(own, F32), ((own_rows, 1), F32), (own, F32), spread],
        reduce_scratch(n, own_rows, width) + chain_sems(n),
        2 * total_rows * local * width,
        context,
        proj_full,
        inputs,
        branch_bias[0, 0:1],
        norm_gain[0, 0:1],
        norm_bias[0, 0:1],
    )
    middle_rows = middle_rows.reshape(total_rows, width)
    pre_act = jnp.dot(middle_rows, up_full, preferred_element_type=F32) + up_bias[0]
    active = gelu_value(pre_act).astype(BF)
    hidden, dres_two, sums_two, dres_two_all = run(
        functools.partial(turn_kernel, n),
        2,
        [(own, F32), (own, F32), sums, spread],
        reduce_scratch(n, own_rows, width) + chain_sems(n),
        2 * total_rows * width * active.shape[1],
        active,
        down_full,
        middle,
        branch_bias[0, 1:2],
        norm_gain[0, 1:2],
        norm_bias[0, 1:2],
        cotangent,
    )
    dres_two_all = dres_two_all.reshape(total_rows, width)
    dpre = jnp.einsum(
        "rd,fd->rf", dres_two_all, down_full, preferred_element_type=F32
    ) * gelu_slope(pre_act)
    upbias_part = jnp.sum(dpre, axis=0)
    dpre_b = dpre.astype(BF)
    down_part = jnp.einsum("rd,rf->df", dres_two_all, active, preferred_element_type=F32)
    up_part = jnp.einsum("rd,rf->df", middle_rows, dpre_b, preferred_element_type=F32)
    units = active.shape[1]
    shard = width // dp
    dres_one, sums_one, dres_one_all, up_out, down_turned = run(
        functools.partial(mid_back_kernel, n, dp),
        3,
        [(own, F32), sums, spread, ((shard, units), F32), ((shard, units), F32)],
        reduce_scratch(n, own_rows, width)
        + chain_sems(n)
        + [pltpu.VMEM((dp, shard, units), BF)] * 2
        + [pltpu.SemaphoreType.DMA((2, dp))] * 2,
        2 * total_rows * width * dpre_b.shape[1],
        dpre_b,
        up_full,
        dres_two,
        normed_one,
        inverse_one,
        norm_gain[0, 0:1],
        up_part.astype(BF).reshape(dp, shard, units),
        down_part.astype(BF).reshape(dp, shard, units),
    )
    dres_one_all = dres_one_all.reshape(total_rows, width)
    proj_part = jnp.einsum("rd,rc->dc", dres_one_all, context, preferred_element_type=F32)
    dcontext = (
        jnp.einsum("rd,cd->rc", dres_one_all, proj_full, preferred_element_type=F32)
        .astype(BF)
        .reshape(head_shape)
    )
    scores = score_block(queries, key_rows, key_valid)
    probs_full = jnp.exp(scores - log_total)
    dprob = jnp.einsum("sqhc,skhc->shqk", dcontext, values, preferred_element_type=F32)
    dscore = (
        probs_full
        * (dprob - jnp.sum(probs_full * dprob, axis=-1, keepdims=True))
        * (1.0 / math.sqrt(HD))
    ).astype(BF)
    dquery = jnp.einsum("shqk,skhc->sqhc", dscore, key_rows, preferred_element_type=F32)
    dkey = jnp.einsum("shqk,sqhc->skhc", dscore, queries, preferred_element_type=F32)
    dvalue = jnp.einsum("shqk,sqhc->skhc", probs_full.astype(BF), dcontext, preferred_element_type=F32)
    dmixed_full = jnp.stack([dquery, dkey, dvalue]).reshape(3, total_rows, local)
    qvbias_part = jnp.stack([jnp.sum(dmixed_full[0], axis=0), jnp.sum(dmixed_full[2], axis=0)])
    dmixed = dmixed_full.astype(BF)
    qkv_part = jnp.dot(
        rounded.T,
        dmixed.transpose(1, 0, 2).reshape(total_rows, 3 * local),
        preferred_element_type=F32,
    )
    all_sums = jnp.concatenate([sums_one, sums_two], axis=0)
    biases = jnp.concatenate([qvbias_part.reshape(1, -1), upbias_part.reshape(1, -1)], axis=1)
    upstream, qkv_turned, proj_turned, all_sums, biases = run(
        functools.partial(last_kernel, n, dp),
        4,
        [
            (own, F32),
            ((shard, 3 * local), F32),
            ((shard, local), F32),
            (all_sums.shape, F32),
            (biases.shape, F32),
        ],
        reduce_scratch(n, own_rows, width)
        + [pltpu.VMEM((dp, shard, 3 * local), BF), pltpu.VMEM((dp, shard, local), BF)]
        + [pltpu.SemaphoreType.DMA((4, dp))] * 2
        + [
            pltpu.VMEM((dp,) + all_sums.shape, F32),
            pltpu.VMEM((dp,) + biases.shape, F32),
            pltpu.VMEM((n,) + all_sums.shape, F32),
        ]
        + [pltpu.SemaphoreType.DMA((1, n))] * 2,
        6 * total_rows * local * width,
        dmixed,
        qkv_full,
        dres_one,
        qkv_part.astype(BF).reshape(dp, shard, 3 * local),
        proj_part.astype(BF).reshape(dp, shard, local),
        all_sums,
        biases,
    )
    qkv_out = qkv_turned.reshape(shard, 3, local).transpose(1, 0, 2)
    proj_out = proj_turned.T
    down_out = down_turned.T
    qvbias_out = biases[0, : 2 * local].reshape(2, local)
    upbias_out = biases[0, 2 * local :]
    pairs = all_sums.reshape(2, 3, width)
    gain_out, normbias_out, branch_out = pairs[:, 0], pairs[:, 1], pairs[:, 2]
    return (
        hidden,
        upstream,
        qkv_out[None],
        qvbias_out[None],
        proj_out[None],
        branch_out[None],
        up_out[None],
        upbias_out[None],
        down_out[None],
        gain_out[None],
        normbias_out[None],
    )


def solution(mesh):
    placed = (
        P(("dp", "tensor"), None),
        P("dp"),
        P(None, None, "dp", "tensor"),
        P(None, None, "tensor"),
        P(None, "tensor", "dp"),
        P(),
        P(None, "dp", "tensor"),
        P(None, "tensor"),
        P(None, "tensor", "dp"),
        P(),
        P(),
        P(("dp", "tensor"), None),
    )
    return jax.shard_map(
        per_device,
        mesh=mesh,
        in_specs=placed,
        out_specs=(
            P(("dp", "tensor"), None),
            P(("dp", "tensor"), None),
            P(None, None, "dp", "tensor"),
            P(None, None, "tensor"),
            P(None, "tensor", "dp"),
            P(),
            P(None, "dp", "tensor"),
            P(None, "tensor"),
            P(None, "tensor", "dp"),
            P(),
            P(),
        ),
        check_vma=False,
    )
```

```python
import functools
import math

import jax
import jax.numpy as jnp
from jax import lax
from jax.experimental import pallas as pl
from jax.experimental.pallas import tpu as pltpu
from jax.sharding import PartitionSpec as P

MESH = pl.DeviceIdType.MESH
BF = jnp.bfloat16
F32 = jnp.float32
HD = 64
L = 512
LAYERS = 1


norm_eps = 1e-12
half_root = 0.7071067811865476
inv_root = 0.3989422804014327


def layer_norm(residual):
    centred = residual - jnp.mean(residual, axis=-1, keepdims=True)
    inverse = lax.rsqrt(jnp.mean(centred * centred, axis=-1, keepdims=True) + norm_eps)
    return (centred * inverse, inverse)


def norm_back(upstream, normed, inverse, gain_row):
    scaled = upstream * gain_row
    return inverse * (
        scaled
        - jnp.mean(scaled, axis=-1, keepdims=True)
        - normed * jnp.mean(scaled * normed, axis=-1, keepdims=True)
    )


def gelu_value(pre_act):
    return 0.5 * pre_act * (1.0 + lax.erf(pre_act * half_root))


def gelu_slope(pre_act):
    return (
        0.5 * (1.0 + lax.erf(pre_act * half_root))
        + pre_act * jnp.exp(-0.5 * pre_act * pre_act) * inv_root
    )


def score_block(queries, key_rows, key_valid):
    raw_scores = jnp.einsum(
        "sqhc,skhc->shqk", queries, key_rows, preferred_element_type=jnp.float32
    ) * (1.0 / math.sqrt(HD))
    return jnp.where(key_valid[:, None, None, :], raw_scores, -1e30)


def send(src, dst, send_sem, recv_sem, axis, target):
    return pltpu.make_async_remote_copy(
        src_ref=src,
        dst_ref=dst,
        send_sem=send_sem,
        recv_sem=recv_sem,
        device_id={axis: target},
        device_id_type=MESH,
    )


def chain_barrier(me, n, extra=0):
    barrier = pltpu.get_barrier_semaphore()

    @pl.when(me > 0)
    def _():
        pl.semaphore_signal(barrier, inc=1, device_id={"tensor": me - 1}, device_id_type=MESH)

    @pl.when(me < n - 1)
    def _():
        pl.semaphore_signal(barrier, inc=1, device_id={"tensor": me + 1}, device_id_type=MESH)

    inner = jnp.logical_and(me > 0, me < n - 1)

    @pl.when(inner)
    def _():
        pl.semaphore_wait(barrier, 2 + extra)

    @pl.when(jnp.logical_not(inner))
    def _():
        pl.semaphore_wait(barrier, 1 + extra)


def group_signal(axis, size):
    mine = lax.axis_index(axis)
    for k in range(1, size):
        pl.semaphore_signal(
            pltpu.get_barrier_semaphore(),
            inc=1,
            device_id={axis: lax.rem(mine + k, size)},
            device_id_type=MESH,
        )


def owners_copy(part, got, ssem, rsem, slot, dp, k):
    target = lax.rem(lax.axis_index("dp") + k, dp)
    return send(part.at[target], got.at[k], ssem.at[slot, k], rsem.at[slot, k], "dp", target)


def owners_sum(parts, gots, outs, ssem, rsem, dp):
    mine = lax.axis_index("dp")
    for slot, (part, got, out) in enumerate(zip(parts, gots, outs)):
        out[...] = part[mine].astype(F32)
        for k in range(1, dp):
            owners_copy(part, got, ssem, rsem, slot, dp, k).wait()
            out[...] += got[k].astype(F32)


def share_copy(got, ssem, rsem, slot, axis, size, k):
    mine = lax.axis_index(axis)
    target = lax.rem(mine + k, size)
    return send(got.at[mine], got.at[mine], ssem.at[slot, k], rsem.at[slot, k], axis, target)


def share_sum(got, ssem, rsem, slot, axis, size):
    for k in range(1, size):
        share_copy(got, ssem, rsem, slot, axis, size, k).wait()
    total = got[0]
    for k in range(1, size):
        total = total + got[k]
    return total


def ways(me, n):
    return ((0, me, me + 1), (1, n - 1 - me, me - 1))


def chain_reduce(term, me, n, acc, tmp, sbuf, rbuf, ssem, rsem):
    def link(way, s, target):
        return send(
            sbuf.at[way, s], rbuf.at[way, s], ssem.at[way, s], rsem.at[way, s], "tensor", target
        )

    for s in range(n - 1):
        for way, pos, target in ways(me, n):
            owner = n - 1 - s + pos
            block = owner if way == 0 else n - 1 - owner

            @pl.when(pos <= s)
            def _(way=way, pos=pos, target=target, block=block):
                tmp[...] = term(block)
                if s > 0:

                    @pl.when(pos > 0)
                    def _():
                        link(way, s - 1, target).wait_recv()
                        tmp[...] += rbuf[way, s - 1].astype(F32)

                sbuf[way, s] = tmp[...].astype(BF)
                link(way, s, target).start()

    acc[...] = term(me)
    for way, pos, target in ways(me, n):

        @pl.when(pos > 0)
        def _(way=way, target=target):
            link(way, n - 2, target).wait_recv()
            acc[...] += rbuf[way, n - 2].astype(F32)

    def finish():
        for s in range(n - 1):
            for way, pos, target in ways(me, n):

                @pl.when(pos <= s)
                def _(way=way, target=target):
                    link(way, s, target).wait_send()

    return finish


def chain_gather(out, me, n, ssem, rsem, between=None):
    def link(way, s, pos, target):
        block = pos - s
        block = block if way == 0 else n - 1 - block
        return send(
            out.at[block], out.at[block], ssem.at[way, s], rsem.at[way, s], "tensor", target
        )

    for s in range(n - 1):
        for way, pos, target in ways(me, n):

            @pl.when(jnp.logical_and(pos >= s, pos < n - 1))
            def _(way=way, pos=pos, target=target):
                if s > 0:
                    link(way, s - 1, pos - 1, target).wait_recv()
                link(way, s, pos, target).start()

        if s == 0 and between is not None:
            between()
    for way, pos, target in ways(me, n):

        @pl.when(pos == n - 1)
        def _(way=way, pos=pos, target=target):
            for s in range(n - 1):
                link(way, s, pos - 1, target).wait_recv()

    for s in range(n - 1):
        for way, pos, target in ways(me, n):

            @pl.when(jnp.logical_and(pos >= s, pos < n - 1))
            def _(way=way, pos=pos, target=target):
                link(way, s, pos, target).wait_send()


def row_block(ref, block, rows):
    return ref[pl.ds(pl.multiple_of(block * rows, rows), rows), :]


def nt_dot(left, right):
    return lax.dot_general(left, right, (((1,), (1,)), ((), ())), preferred_element_type=F32)


def front_kernel(n, dp, x_ref, qkv_ref, proj_ref, rows_ref, qkv_all, proj_all, gs, gr, ws, wr):
    me = lax.axis_index("tensor")
    mine = lax.axis_index("dp")
    barrier = pltpu.get_barrier_semaphore()
    for k in range(1, dp):
        pl.semaphore_signal(
            barrier, inc=1, device_id={"dp": lax.rem(mine + k, dp)}, device_id_type=MESH
        )
    chain_barrier(me, n, dp - 1)

    def links(k):
        target = lax.rem(mine + k, dp)
        return (
            send(qkv_ref, qkv_all.at[mine], ws.at[0, k], wr.at[0, k], "dp", target),
            send(proj_ref, proj_all.at[mine], ws.at[1, k], wr.at[1, k], "dp", target),
        )

    rows_ref[me] = x_ref[...].astype(BF)

    def between():
        for k in range(1, dp):
            for copy in links(k):
                copy.start()
        qkv_all[mine] = qkv_ref[...]
        proj_all[mine] = proj_ref[...]

    chain_gather(rows_ref, me, n, gs, gr, between)
    for k in range(1, dp):
        for copy in links(k):
            copy.wait()


def attn_out_kernel(
    n, ctx, proj, hidden, bias, gain, nbias,
    normed_o, inv_o, middle_o, rows_o,
    acc, tmp, sbuf, rbuf, ss, sr, gs, gr,
):
    me = lax.axis_index("tensor")
    rows = hidden.shape[0]
    chain_barrier(me, n)
    finish = chain_reduce(
        lambda block: jnp.dot(row_block(ctx, block, rows), proj[...], preferred_element_type=F32),
        me, n, acc, tmp, sbuf, rbuf, ss, sr,
    )
    normed, inverse = layer_norm(hidden[...] + acc[...] + bias[...])
    middle = normed * gain[...] + nbias[...]
    normed_o[...] = normed
    inv_o[...] = inverse
    middle_o[...] = middle
    rows_o[me] = middle.astype(BF)
    chain_gather(rows_o, me, n, gs, gr)
    finish()


def turn_kernel(
    n, act, down, middle, bias, gain, nbias, cot,
    hidden_o, dres_o, sums_o, rows_o,
    acc, tmp, sbuf, rbuf, ss, sr, gs, gr,
):
    me = lax.axis_index("tensor")
    rows = middle.shape[0]
    chain_barrier(me, n)
    finish = chain_reduce(
        lambda block: jnp.dot(row_block(act, block, rows), down[...], preferred_element_type=F32),
        me, n, acc, tmp, sbuf, rbuf, ss, sr,
    )
    normed, inverse = layer_norm(middle[...] + acc[...] + bias[...])
    acc[...] = normed
    dres = norm_back(cot[...], normed, inverse, gain[...])
    dres_o[...] = dres
    rows_o[me] = dres.astype(BF)

    def between():
        hidden_o[...] = acc[...] * gain[...] + nbias[...]
        sums_o[0:1, :] = jnp.sum(cot[...] * acc[...], axis=0, keepdims=True)
        sums_o[1:2, :] = jnp.sum(cot[...], axis=0, keepdims=True)
        sums_o[2:3, :] = jnp.sum(dres_o[...], axis=0, keepdims=True)

    chain_gather(rows_o, me, n, gs, gr, between)
    finish()


def mid_back_kernel(
    n, dp, dpre, up, dres_two, normed, inverse, gain, up_part, down_part,
    dres_o, sums_o, rows_o, up_o, down_o,
    acc, tmp, sbuf, rbuf, ss, sr, gs, gr, up_got, down_got, ws, wr,
):
    me = lax.axis_index("tensor")
    rows = normed.shape[0]
    group_signal("dp", dp)
    chain_barrier(me, n, dp - 1)
    parts, gots, outs = (up_part, down_part), (up_got, down_got), (up_o, down_o)
    for k in range(1, dp):
        for slot in range(2):
            owners_copy(parts[slot], gots[slot], ws, wr, slot, dp, k).start()
    finish = chain_reduce(
        lambda block: nt_dot(row_block(dpre, block, rows), up[...]),
        me, n, acc, tmp, sbuf, rbuf, ss, sr,
    )
    acc[...] += dres_two[...]
    dres = norm_back(acc[...], normed[...], inverse[...], gain[...])
    dres_o[...] = dres
    rows_o[me] = dres.astype(BF)

    def between():
        sums_o[0:1, :] = jnp.sum(acc[...] * normed[...], axis=0, keepdims=True)
        sums_o[1:2, :] = jnp.sum(acc[...], axis=0, keepdims=True)
        sums_o[2:3, :] = jnp.sum(dres_o[...], axis=0, keepdims=True)

    chain_gather(rows_o, me, n, gs, gr, between)
    finish()
    owners_sum(parts, gots, outs, ws, wr, dp)


def tn_dot(left, right):
    return lax.dot_general(left, right, (((0,), (0,)), ((), ())), preferred_element_type=F32)


def attn_back_kernel(
    lengths, dres, proj, ctx, rounded, query, keyrow, value,
    dmix_o, qkv_o, proj_o, bias_o, dctx,
):
    local = ctx.shape[1]
    scale = 1.0 / math.sqrt(HD)
    dctx[...] = nt_dot(dres[...], proj[...]).astype(BF)
    proj_o[...] = tn_dot(dres[...], ctx[...]).astype(BF)
    for seq in range(ctx.shape[0] // L):
        rows = slice(seq * L, (seq + 1) * L)
        valid = lax.broadcasted_iota(jnp.int32, (L, L), 1) < lengths[seq]
        for head in range(local // HD):
            cols = slice(head * HD, (head + 1) * HD)
            q, k, v, dc = query[rows, cols], keyrow[rows, cols], value[rows, cols], dctx[rows, cols]
            scores = jnp.where(valid, nt_dot(q, k) * scale, -1e30)
            weights = jnp.exp(scores - jnp.max(scores, axis=-1, keepdims=True))
            prob = weights * (1.0 / jnp.sum(weights, axis=-1, keepdims=True))
            dprob = nt_dot(dc, v)
            inner = jnp.sum(prob * dprob, axis=-1, keepdims=True)
            dscore = (prob * (dprob - inner) * scale).astype(BF)
            grads = (
                jnp.dot(dscore, k, preferred_element_type=F32),
                tn_dot(dscore, q),
                tn_dot(prob.astype(BF), dc),
            )
            for j, grad in enumerate(grads):
                spot = slice(j * local + head * HD, j * local + (head + 1) * HD)
                dmix_o[rows, spot] = grad.astype(BF)
                total = jnp.sum(grad, axis=0, keepdims=True)
                bias_o[:, spot] = total if seq == 0 else bias_o[:, spot] + total
    qkv_o[...] = tn_dot(rounded[...], dmix_o[...]).astype(BF)


def last_kernel(
    n, dp, dmix, qkv, dres, qkv_part, proj_part, sums, biases,
    up_o, qkv_o, proj_o, sums_o, biases_o,
    acc, tmp, sbuf, rbuf, ss, sr, qkv_got, proj_got, ws, wr, sums_got, biases_got, sums_all, ts, tr,
):
    me = lax.axis_index("tensor")
    mine = lax.axis_index("dp")
    rows = dres.shape[0]
    group_signal("dp", dp)
    group_signal("tensor", n)
    pl.semaphore_wait(pltpu.get_barrier_semaphore(), dp + n - 2)
    sums_got[mine] = sums[...]
    biases_got[mine] = biases[...]
    parts, gots, outs = (qkv_part, proj_part), (qkv_got, proj_got), (qkv_o, proj_o)
    for k in range(1, dp):
        share_copy(sums_got, ws, wr, 2, "dp", dp, k).start()
        share_copy(biases_got, ws, wr, 3, "dp", dp, k).start()
    for k in range(1, dp):
        for slot in range(2):
            owners_copy(parts[slot], gots[slot], ws, wr, slot, dp, k).start()

    def term(block):
        return nt_dot(row_block(dmix, block, rows), qkv[...])

    finish = chain_reduce(term, me, n, acc, tmp, sbuf, rbuf, ss, sr)
    sums_all[me] = share_sum(sums_got, ws, wr, 2, "dp", dp)
    for k in range(1, n):
        share_copy(sums_all, ts, tr, 0, "tensor", n, k).start()
    biases_o[...] = share_sum(biases_got, ws, wr, 3, "dp", dp)
    up_o[...] = dres[...] + acc[...]
    owners_sum(parts, gots, outs, ws, wr, dp)
    finish()
    sums_o[...] = share_sum(sums_all, ts, tr, 0, "tensor", n)


def run(body, number, outs, scratch, flops, *operands):
    vmem = pl.BlockSpec(memory_space=pltpu.VMEM)
    return pl.pallas_call(
        body,
        out_shape=[jax.ShapeDtypeStruct(shape, dtype) for shape, dtype in outs],
        in_specs=[vmem] * len(operands),
        out_specs=[vmem] * len(outs),
        scratch_shapes=scratch,
        cost_estimate=pl.CostEstimate(flops=flops, bytes_accessed=60_000_000, transcendentals=0),
        compiler_params=pltpu.CompilerParams(
            collective_id=number, has_side_effects=True, vmem_limit_bytes=40 * 2**20
        ),
    )(*operands)


def reduce_scratch(n, rows, width):
    return [
        pltpu.VMEM((rows, width), F32),
        pltpu.VMEM((rows, width), F32),
        pltpu.VMEM((2, n - 1, rows, width), BF),
        pltpu.VMEM((2, n - 1, rows, width), BF),
    ] + chain_sems(n)


def chain_sems(n):
    return [pltpu.SemaphoreType.DMA((2, n - 1)), pltpu.SemaphoreType.DMA((2, n - 1))]


def per_device(
    inputs,
    lengths,
    qkv_weight,
    qv_bias,
    proj_weight,
    branch_bias,
    up_weight,
    up_bias,
    down_weight,
    norm_gain,
    norm_bias,
    cotangent,
):
    n = lax.axis_size("tensor")
    dp = lax.axis_size("dp")
    own_rows, width = inputs.shape
    seq_count = lengths.shape[0]
    local = qkv_weight.shape[3]
    head_count = local // HD
    head_shape = (seq_count, L, head_count, HD)
    key_valid = jnp.arange(L, dtype=jnp.int32)[None, :] < lengths[:, None]
    total_rows = own_rows * n
    own = (own_rows, width)
    spread = ((n, own_rows, width), BF)
    sums = ((3, width), F32)
    up_full = lax.all_gather(up_weight[0], "dp", axis=0, tiled=True)
    down_full = lax.all_gather(down_weight[0], "dp", axis=1, tiled=True)
    rounded, qkv_blocks, proj_blocks = run(
        functools.partial(front_kernel, n, dp),
        0,
        [spread, ((dp,) + qkv_weight.shape[1:], BF), ((dp,) + proj_weight.shape[1:], BF)],
        chain_sems(n)
        + [pltpu.SemaphoreType.DMA((2, dp)), pltpu.SemaphoreType.DMA((2, dp))],
        0,
        inputs,
        qkv_weight[0],
        proj_weight[0],
    )
    rounded = rounded.reshape(total_rows, width)
    qkv_full = qkv_blocks.transpose(0, 2, 1, 3).reshape(width, 3 * local)
    proj_full = proj_blocks.transpose(1, 0, 2).reshape(local, width)
    mixed_rows = jnp.dot(rounded, qkv_full, preferred_element_type=F32)
    queries_2d = (mixed_rows[:, :local] + qv_bias[0, 0]).astype(BF)
    key_2d = mixed_rows[:, local : 2 * local].astype(BF)
    values_2d = (mixed_rows[:, 2 * local :] + qv_bias[0, 1]).astype(BF)
    queries = queries_2d.reshape(head_shape)
    key_rows = key_2d.reshape(head_shape)
    values = values_2d.reshape(head_shape)
    scores = score_block(queries, key_rows, key_valid)
    row_peak = jnp.max(scores, axis=-1, keepdims=True)
    log_total = row_peak + jnp.log(jnp.sum(jnp.exp(scores - row_peak), axis=-1, keepdims=True))
    soft_weights = jnp.exp(scores - log_total).astype(BF)
    context = (
        jnp.einsum("shqk,skhc->sqhc", soft_weights, values, preferred_element_type=F32)
        .astype(BF)
        .reshape(total_rows, local)
    )
    normed_one, inverse_one, middle, middle_rows = run(
        functools.partial(attn_out_kernel, n),
        1,
        [(own, F32), ((own_rows, 1), F32), (own, F32), spread],
        reduce_scratch(n, own_rows, width) + chain_sems(n),
        2 * total_rows * local * width,
        context,
        proj_full,
        inputs,
        branch_bias[0, 0:1],
        norm_gain[0, 0:1],
        norm_bias[0, 0:1],
    )
    middle_rows = middle_rows.reshape(total_rows, width)
    pre_act = jnp.dot(middle_rows, up_full, preferred_element_type=F32) + up_bias[0]
    active = gelu_value(pre_act).astype(BF)
    hidden, dres_two, sums_two, dres_two_all = run(
        functools.partial(turn_kernel, n),
        2,
        [(own, F32), (own, F32), sums, spread],
        reduce_scratch(n, own_rows, width) + chain_sems(n),
        2 * total_rows * width * active.shape[1],
        active,
        down_full,
        middle,
        branch_bias[0, 1:2],
        norm_gain[0, 1:2],
        norm_bias[0, 1:2],
        cotangent,
    )
    dres_two_all = dres_two_all.reshape(total_rows, width)
    dpre = jnp.einsum(
        "rd,fd->rf", dres_two_all, down_full, preferred_element_type=F32
    ) * gelu_slope(pre_act)
    upbias_part = jnp.sum(dpre, axis=0)
    dpre_b = dpre.astype(BF)
    down_part = jnp.einsum("rd,rf->df", dres_two_all, active, preferred_element_type=F32)
    up_part = jnp.einsum("rd,rf->df", middle_rows, dpre_b, preferred_element_type=F32)
    units = active.shape[1]
    shard = width // dp
    dres_one, sums_one, dres_one_all, up_out, down_turned = run(
        functools.partial(mid_back_kernel, n, dp),
        3,
        [(own, F32), sums, spread, ((shard, units), F32), ((shard, units), F32)],
        reduce_scratch(n, own_rows, width)
        + chain_sems(n)
        + [pltpu.VMEM((dp, shard, units), BF)] * 2
        + [pltpu.SemaphoreType.DMA((2, dp))] * 2,
        2 * total_rows * width * dpre_b.shape[1],
        dpre_b,
        up_full,
        dres_two,
        normed_one,
        inverse_one,
        norm_gain[0, 0:1],
        up_part.astype(BF).reshape(dp, shard, units),
        down_part.astype(BF).reshape(dp, shard, units),
    )
    dres_one_all = dres_one_all.reshape(total_rows, width)
    vmem = pl.BlockSpec(memory_space=pltpu.VMEM)
    dmixed, qkv_part, proj_part, mix_sums = pl.pallas_call(
        attn_back_kernel,
        out_shape=[
            jax.ShapeDtypeStruct((total_rows, 3 * local), BF),
            jax.ShapeDtypeStruct((width, 3 * local), BF),
            jax.ShapeDtypeStruct((width, local), BF),
            jax.ShapeDtypeStruct((1, 3 * local), F32),
        ],
        in_specs=[pl.BlockSpec(memory_space=pltpu.SMEM)] + [vmem] * 7,
        out_specs=[vmem] * 4,
        scratch_shapes=[pltpu.VMEM((total_rows, local), BF)],
        compiler_params=pltpu.CompilerParams(vmem_limit_bytes=40 * 2**20),
    )(
        lengths, dres_one_all, proj_full, context, rounded, queries_2d, key_2d, values_2d
    )
    all_sums = jnp.concatenate([sums_one, sums_two], axis=0)
    biases = jnp.concatenate([mix_sums, upbias_part.reshape(1, -1)], axis=1)
    upstream, qkv_turned, proj_turned, all_sums, biases = run(
        functools.partial(last_kernel, n, dp),
        4,
        [
            (own, F32),
            ((shard, 3 * local), F32),
            ((shard, local), F32),
            (all_sums.shape, F32),
            (biases.shape, F32),
        ],
        reduce_scratch(n, own_rows, width)
        + [pltpu.VMEM((dp, shard, 3 * local), BF), pltpu.VMEM((dp, shard, local), BF)]
        + [pltpu.SemaphoreType.DMA((4, dp))] * 2
        + [
            pltpu.VMEM((dp,) + all_sums.shape, F32),
            pltpu.VMEM((dp,) + biases.shape, F32),
            pltpu.VMEM((n,) + all_sums.shape, F32),
        ]
        + [pltpu.SemaphoreType.DMA((1, n))] * 2,
        6 * total_rows * local * width,
        dmixed,
        qkv_full,
        dres_one,
        qkv_part.reshape(dp, shard, 3 * local),
        proj_part.reshape(dp, shard, local),
        all_sums,
        biases,
    )
    qkv_out = qkv_turned.reshape(shard, 3, local).transpose(1, 0, 2)
    proj_out = proj_turned.T
    down_out = down_turned.T
    qvbias_out = jnp.stack([biases[0, :local], biases[0, 2 * local : 3 * local]])
    upbias_out = biases[0, 3 * local :]
    pairs = all_sums.reshape(2, 3, width)
    gain_out, normbias_out, branch_out = pairs[:, 0], pairs[:, 1], pairs[:, 2]
    return (
        hidden,
        upstream,
        qkv_out[None],
        qvbias_out[None],
        proj_out[None],
        branch_out[None],
        up_out[None],
        upbias_out[None],
        down_out[None],
        gain_out[None],
        normbias_out[None],
    )


def solution(mesh):
    placed = (
        P(("dp", "tensor"), None),
        P("dp"),
        P(None, None, "dp", "tensor"),
        P(None, None, "tensor"),
        P(None, "tensor", "dp"),
        P(),
        P(None, "dp", "tensor"),
        P(None, "tensor"),
        P(None, "tensor", "dp"),
        P(),
        P(),
        P(("dp", "tensor"), None),
    )
    return jax.shard_map(
        per_device,
        mesh=mesh,
        in_specs=placed,
        out_specs=(
            P(("dp", "tensor"), None),
            P(("dp", "tensor"), None),
            P(None, None, "dp", "tensor"),
            P(None, None, "tensor"),
            P(None, "tensor", "dp"),
            P(),
            P(None, "dp", "tensor"),
            P(None, "tensor"),
            P(None, "tensor", "dp"),
            P(),
            P(),
        ),
        check_vma=False,
    )
```

```python
import functools
import math

import jax
import jax.numpy as jnp
from jax import lax
from jax.experimental import pallas as pl
from jax.experimental.pallas import tpu as pltpu
from jax.sharding import PartitionSpec as P

MESH = pl.DeviceIdType.MESH
BF = jnp.bfloat16
F32 = jnp.float32
HD = 64
L = 512
LAYERS = 1


norm_eps = 1e-12
half_root = 0.7071067811865476
inv_root = 0.3989422804014327


def layer_norm(residual):
    centred = residual - jnp.mean(residual, axis=-1, keepdims=True)
    inverse = lax.rsqrt(jnp.mean(centred * centred, axis=-1, keepdims=True) + norm_eps)
    return (centred * inverse, inverse)


def norm_back(upstream, normed, inverse, gain_row):
    scaled = upstream * gain_row
    return inverse * (
        scaled
        - jnp.mean(scaled, axis=-1, keepdims=True)
        - normed * jnp.mean(scaled * normed, axis=-1, keepdims=True)
    )


def gelu_value(pre_act):
    return 0.5 * pre_act * (1.0 + lax.erf(pre_act * half_root))


def gelu_slope(pre_act):
    return (
        0.5 * (1.0 + lax.erf(pre_act * half_root))
        + pre_act * jnp.exp(-0.5 * pre_act * pre_act) * inv_root
    )


def send(src, dst, send_sem, recv_sem, axis, target):
    return pltpu.make_async_remote_copy(
        src_ref=src,
        dst_ref=dst,
        send_sem=send_sem,
        recv_sem=recv_sem,
        device_id={axis: target},
        device_id_type=MESH,
    )


def chain_barrier(me, n, extra=0):
    barrier = pltpu.get_barrier_semaphore()

    @pl.when(me > 0)
    def _():
        pl.semaphore_signal(barrier, inc=1, device_id={"tensor": me - 1}, device_id_type=MESH)

    @pl.when(me < n - 1)
    def _():
        pl.semaphore_signal(barrier, inc=1, device_id={"tensor": me + 1}, device_id_type=MESH)

    inner = jnp.logical_and(me > 0, me < n - 1)

    @pl.when(inner)
    def _():
        pl.semaphore_wait(barrier, 2 + extra)

    @pl.when(jnp.logical_not(inner))
    def _():
        pl.semaphore_wait(barrier, 1 + extra)


def group_signal(axis, size):
    mine = lax.axis_index(axis)
    for k in range(1, size):
        pl.semaphore_signal(
            pltpu.get_barrier_semaphore(),
            inc=1,
            device_id={axis: lax.rem(mine + k, size)},
            device_id_type=MESH,
        )


def owners_copy(part, got, ssem, rsem, slot, dp, k):
    target = lax.rem(lax.axis_index("dp") + k, dp)
    return send(part.at[target], got.at[k], ssem.at[slot, k], rsem.at[slot, k], "dp", target)


def owners_sum(parts, gots, outs, ssem, rsem, dp):
    mine = lax.axis_index("dp")
    for slot, (part, got, out) in enumerate(zip(parts, gots, outs)):
        out[...] = part[mine].astype(F32)
        for k in range(1, dp):
            owners_copy(part, got, ssem, rsem, slot, dp, k).wait()
            out[...] += got[k].astype(F32)


def share_copy(got, ssem, rsem, slot, axis, size, k):
    mine = lax.axis_index(axis)
    target = lax.rem(mine + k, size)
    return send(got.at[mine], got.at[mine], ssem.at[slot, k], rsem.at[slot, k], axis, target)


def share_sum(got, ssem, rsem, slot, axis, size):
    for k in range(1, size):
        share_copy(got, ssem, rsem, slot, axis, size, k).wait()
    total = got[0]
    for k in range(1, size):
        total = total + got[k]
    return total


def ways(me, n):
    return ((0, me, me + 1), (1, n - 1 - me, me - 1))


def chain_reduce(term, me, n, acc, tmp, sbuf, rbuf, ssem, rsem):
    def link(way, s, target):
        return send(
            sbuf.at[way, s], rbuf.at[way, s], ssem.at[way, s], rsem.at[way, s], "tensor", target
        )

    for s in range(n - 1):
        for way, pos, target in ways(me, n):
            owner = n - 1 - s + pos
            block = owner if way == 0 else n - 1 - owner

            @pl.when(pos <= s)
            def _(way=way, pos=pos, target=target, block=block):
                tmp[...] = term(block)
                if s > 0:

                    @pl.when(pos > 0)
                    def _():
                        link(way, s - 1, target).wait_recv()
                        tmp[...] += rbuf[way, s - 1].astype(F32)

                sbuf[way, s] = tmp[...].astype(BF)
                link(way, s, target).start()

    acc[...] = term(me)
    for way, pos, target in ways(me, n):

        @pl.when(pos > 0)
        def _(way=way, target=target):
            link(way, n - 2, target).wait_recv()
            acc[...] += rbuf[way, n - 2].astype(F32)

    def finish():
        for s in range(n - 1):
            for way, pos, target in ways(me, n):

                @pl.when(pos <= s)
                def _(way=way, target=target):
                    link(way, s, target).wait_send()

    return finish


def chain_gather(out, me, n, ssem, rsem, between=None):
    def link(way, s, pos, target):
        block = pos - s
        block = block if way == 0 else n - 1 - block
        return send(
            out.at[block], out.at[block], ssem.at[way, s], rsem.at[way, s], "tensor", target
        )

    for s in range(n - 1):
        for way, pos, target in ways(me, n):

            @pl.when(jnp.logical_and(pos >= s, pos < n - 1))
            def _(way=way, pos=pos, target=target):
                if s > 0:
                    link(way, s - 1, pos - 1, target).wait_recv()
                link(way, s, pos, target).start()

        if s == 0 and between is not None:
            between()
    for way, pos, target in ways(me, n):

        @pl.when(pos == n - 1)
        def _(way=way, pos=pos, target=target):
            for s in range(n - 1):
                link(way, s, pos - 1, target).wait_recv()

    for s in range(n - 1):
        for way, pos, target in ways(me, n):

            @pl.when(jnp.logical_and(pos >= s, pos < n - 1))
            def _(way=way, pos=pos, target=target):
                link(way, s, pos, target).wait_send()


def row_block(ref, block, rows):
    return ref[pl.ds(pl.multiple_of(block * rows, rows), rows), :]


def nt_dot(left, right):
    return lax.dot_general(left, right, (((1,), (1,)), ((), ())), preferred_element_type=F32)


def front_kernel(n, dp, x_ref, qkv_ref, proj_ref, rows_ref, qkv_all, proj_all, gs, gr, ws, wr):
    me = lax.axis_index("tensor")
    mine = lax.axis_index("dp")
    barrier = pltpu.get_barrier_semaphore()
    for k in range(1, dp):
        pl.semaphore_signal(
            barrier, inc=1, device_id={"dp": lax.rem(mine + k, dp)}, device_id_type=MESH
        )
    chain_barrier(me, n, dp - 1)

    def links(k):
        target = lax.rem(mine + k, dp)
        return (
            send(qkv_ref, qkv_all.at[mine], ws.at[0, k], wr.at[0, k], "dp", target),
            send(proj_ref, proj_all.at[mine], ws.at[1, k], wr.at[1, k], "dp", target),
        )

    rows_ref[me] = x_ref[...].astype(BF)

    def between():
        for k in range(1, dp):
            for copy in links(k):
                copy.start()
        qkv_all[mine] = qkv_ref[...]
        proj_all[mine] = proj_ref[...]

    chain_gather(rows_ref, me, n, gs, gr, between)
    for k in range(1, dp):
        for copy in links(k):
            copy.wait()


def attn_out_kernel(
    n, ctx, proj, hidden, bias, gain, nbias,
    normed_o, inv_o, middle_o, rows_o,
    acc, tmp, sbuf, rbuf, ss, sr, gs, gr,
):
    me = lax.axis_index("tensor")
    rows = hidden.shape[0]
    chain_barrier(me, n)
    finish = chain_reduce(
        lambda block: jnp.dot(row_block(ctx, block, rows), proj[...], preferred_element_type=F32),
        me, n, acc, tmp, sbuf, rbuf, ss, sr,
    )
    normed, inverse = layer_norm(hidden[...] + acc[...] + bias[...])
    middle = normed * gain[...] + nbias[...]
    normed_o[...] = normed
    inv_o[...] = inverse
    middle_o[...] = middle
    rows_o[me] = middle.astype(BF)
    chain_gather(rows_o, me, n, gs, gr)
    finish()


def turn_kernel(
    n, act, down, middle, bias, gain, nbias, cot,
    hidden_o, dres_o, sums_o, rows_o,
    acc, tmp, sbuf, rbuf, ss, sr, gs, gr,
):
    me = lax.axis_index("tensor")
    rows = middle.shape[0]
    chain_barrier(me, n)
    finish = chain_reduce(
        lambda block: jnp.dot(row_block(act, block, rows), down[...], preferred_element_type=F32),
        me, n, acc, tmp, sbuf, rbuf, ss, sr,
    )
    normed, inverse = layer_norm(middle[...] + acc[...] + bias[...])
    acc[...] = normed
    dres = norm_back(cot[...], normed, inverse, gain[...])
    dres_o[...] = dres
    rows_o[me] = dres.astype(BF)

    def between():
        hidden_o[...] = acc[...] * gain[...] + nbias[...]
        sums_o[0:1, :] = jnp.sum(cot[...] * acc[...], axis=0, keepdims=True)
        sums_o[1:2, :] = jnp.sum(cot[...], axis=0, keepdims=True)
        sums_o[2:3, :] = jnp.sum(dres_o[...], axis=0, keepdims=True)

    chain_gather(rows_o, me, n, gs, gr, between)
    finish()


def mid_back_kernel(
    n, dp, dpre, up, dres_two, normed, inverse, gain, up_part, down_part,
    dres_o, sums_o, rows_o, up_o, down_o,
    acc, tmp, sbuf, rbuf, ss, sr, gs, gr, up_got, down_got, ws, wr,
):
    me = lax.axis_index("tensor")
    rows = normed.shape[0]
    group_signal("dp", dp)
    chain_barrier(me, n, dp - 1)
    parts, gots, outs = (up_part, down_part), (up_got, down_got), (up_o, down_o)
    for k in range(1, dp):
        for slot in range(2):
            owners_copy(parts[slot], gots[slot], ws, wr, slot, dp, k).start()
    finish = chain_reduce(
        lambda block: nt_dot(row_block(dpre, block, rows), up[...]),
        me, n, acc, tmp, sbuf, rbuf, ss, sr,
    )
    acc[...] += dres_two[...]
    dres = norm_back(acc[...], normed[...], inverse[...], gain[...])
    dres_o[...] = dres
    rows_o[me] = dres.astype(BF)

    def between():
        sums_o[0:1, :] = jnp.sum(acc[...] * normed[...], axis=0, keepdims=True)
        sums_o[1:2, :] = jnp.sum(acc[...], axis=0, keepdims=True)
        sums_o[2:3, :] = jnp.sum(dres_o[...], axis=0, keepdims=True)

    chain_gather(rows_o, me, n, gs, gr, between)
    finish()
    owners_sum(parts, gots, outs, ws, wr, dp)


def tn_dot(left, right):
    return lax.dot_general(left, right, (((0,), (0,)), ((), ())), preferred_element_type=F32)


def attn_kernel(
    lengths, rounded, qkv_all, proj_all, bias,
    query, keyrow, value, ctx, qkv_o, proj_o,
):
    dp, local, shard = proj_all.shape
    scale = 1.0 / math.sqrt(HD)
    for d in range(dp):
        part = slice(d * shard, (d + 1) * shard)
        for j in range(3):
            qkv_o[part, j * local : (j + 1) * local] = qkv_all[d, j]
        proj_o[:, part] = proj_all[d]
    mixed = jnp.dot(rounded[...], qkv_o[...], preferred_element_type=F32)
    query[...] = (mixed[:, :local] + bias[0:1, :]).astype(BF)
    keyrow[...] = mixed[:, local : 2 * local].astype(BF)
    value[...] = (mixed[:, 2 * local :] + bias[1:2, :]).astype(BF)
    for seq in range(ctx.shape[0] // L):
        rows = slice(seq * L, (seq + 1) * L)
        valid = lax.broadcasted_iota(jnp.int32, (L, L), 1) < lengths[seq]
        for head in range(local // HD):
            cols = slice(head * HD, (head + 1) * HD)
            scores = nt_dot(query[rows, cols], keyrow[rows, cols]) * scale
            scores = jnp.where(valid, scores, -1e30)
            weights = jnp.exp(scores - jnp.max(scores, axis=-1, keepdims=True))
            prob = weights * (1.0 / jnp.sum(weights, axis=-1, keepdims=True))
            ctx[rows, cols] = jnp.dot(
                prob.astype(BF), value[rows, cols], preferred_element_type=F32
            ).astype(BF)


def attn_back_kernel(
    lengths, dres, proj, ctx, rounded, query, keyrow, value,
    dmix_o, qkv_o, proj_o, bias_o, dctx,
):
    local = ctx.shape[1]
    scale = 1.0 / math.sqrt(HD)
    dctx[...] = nt_dot(dres[...], proj[...]).astype(BF)
    proj_o[...] = tn_dot(dres[...], ctx[...]).astype(BF)
    for seq in range(ctx.shape[0] // L):
        rows = slice(seq * L, (seq + 1) * L)
        valid = lax.broadcasted_iota(jnp.int32, (L, L), 1) < lengths[seq]
        for head in range(local // HD):
            cols = slice(head * HD, (head + 1) * HD)
            q, k, v, dc = query[rows, cols], keyrow[rows, cols], value[rows, cols], dctx[rows, cols]
            scores = jnp.where(valid, nt_dot(q, k) * scale, -1e30)
            weights = jnp.exp(scores - jnp.max(scores, axis=-1, keepdims=True))
            prob = weights * (1.0 / jnp.sum(weights, axis=-1, keepdims=True))
            dprob = nt_dot(dc, v)
            inner = jnp.sum(prob * dprob, axis=-1, keepdims=True)
            dscore = (prob * (dprob - inner) * scale).astype(BF)
            grads = (
                jnp.dot(dscore, k, preferred_element_type=F32),
                tn_dot(dscore, q),
                tn_dot(prob.astype(BF), dc),
            )
            for j, grad in enumerate(grads):
                spot = slice(j * local + head * HD, j * local + (head + 1) * HD)
                dmix_o[rows, spot] = grad.astype(BF)
                total = jnp.sum(grad, axis=0, keepdims=True)
                bias_o[:, spot] = total if seq == 0 else bias_o[:, spot] + total
    qkv_o[...] = tn_dot(rounded[...], dmix_o[...]).astype(BF)


def last_kernel(
    n, dp, dmix, qkv, dres, qkv_part, proj_part, sums, biases,
    up_o, qkv_o, proj_o, sums_o, biases_o,
    acc, tmp, sbuf, rbuf, ss, sr, qkv_got, proj_got, ws, wr, sums_got, biases_got, sums_all, ts, tr,
):
    me = lax.axis_index("tensor")
    mine = lax.axis_index("dp")
    rows = dres.shape[0]
    group_signal("dp", dp)
    group_signal("tensor", n)
    pl.semaphore_wait(pltpu.get_barrier_semaphore(), dp + n - 2)
    sums_got[mine] = sums[...]
    biases_got[mine] = biases[...]
    parts, gots, outs = (qkv_part, proj_part), (qkv_got, proj_got), (qkv_o, proj_o)
    for k in range(1, dp):
        share_copy(sums_got, ws, wr, 2, "dp", dp, k).start()
        share_copy(biases_got, ws, wr, 3, "dp", dp, k).start()
    for k in range(1, dp):
        for slot in range(2):
            owners_copy(parts[slot], gots[slot], ws, wr, slot, dp, k).start()

    def term(block):
        return nt_dot(row_block(dmix, block, rows), qkv[...])

    finish = chain_reduce(term, me, n, acc, tmp, sbuf, rbuf, ss, sr)
    sums_all[me] = share_sum(sums_got, ws, wr, 2, "dp", dp)
    for k in range(1, n):
        share_copy(sums_all, ts, tr, 0, "tensor", n, k).start()
    biases_o[...] = share_sum(biases_got, ws, wr, 3, "dp", dp)
    up_o[...] = dres[...] + acc[...]
    owners_sum(parts, gots, outs, ws, wr, dp)
    finish()
    sums_o[...] = share_sum(sums_all, ts, tr, 0, "tensor", n)


def run(body, number, outs, scratch, flops, *operands):
    vmem = pl.BlockSpec(memory_space=pltpu.VMEM)
    return pl.pallas_call(
        body,
        out_shape=[jax.ShapeDtypeStruct(shape, dtype) for shape, dtype in outs],
        in_specs=[vmem] * len(operands),
        out_specs=[vmem] * len(outs),
        scratch_shapes=scratch,
        cost_estimate=pl.CostEstimate(flops=flops, bytes_accessed=60_000_000, transcendentals=0),
        compiler_params=pltpu.CompilerParams(
            collective_id=number, has_side_effects=True, vmem_limit_bytes=40 * 2**20
        ),
    )(*operands)


def reduce_scratch(n, rows, width):
    return [
        pltpu.VMEM((rows, width), F32),
        pltpu.VMEM((rows, width), F32),
        pltpu.VMEM((2, n - 1, rows, width), BF),
        pltpu.VMEM((2, n - 1, rows, width), BF),
    ] + chain_sems(n)


def chain_sems(n):
    return [pltpu.SemaphoreType.DMA((2, n - 1)), pltpu.SemaphoreType.DMA((2, n - 1))]


def per_device(
    inputs,
    lengths,
    qkv_weight,
    qv_bias,
    proj_weight,
    branch_bias,
    up_weight,
    up_bias,
    down_weight,
    norm_gain,
    norm_bias,
    cotangent,
):
    n = lax.axis_size("tensor")
    dp = lax.axis_size("dp")
    own_rows, width = inputs.shape
    local = qkv_weight.shape[3]
    total_rows = own_rows * n
    own = (own_rows, width)
    spread = ((n, own_rows, width), BF)
    sums = ((3, width), F32)
    up_full = lax.all_gather(up_weight[0], "dp", axis=0, tiled=True)
    down_full = lax.all_gather(down_weight[0], "dp", axis=1, tiled=True)
    rounded, qkv_blocks, proj_blocks = run(
        functools.partial(front_kernel, n, dp),
        0,
        [spread, ((dp,) + qkv_weight.shape[1:], BF), ((dp,) + proj_weight.shape[1:], BF)],
        chain_sems(n)
        + [pltpu.SemaphoreType.DMA((2, dp)), pltpu.SemaphoreType.DMA((2, dp))],
        0,
        inputs,
        qkv_weight[0],
        proj_weight[0],
    )
    rounded = rounded.reshape(total_rows, width)
    vmem = pl.BlockSpec(memory_space=pltpu.VMEM)
    heads = jax.ShapeDtypeStruct((total_rows, local), BF)
    queries_2d, key_2d, values_2d, context, qkv_full, proj_full = pl.pallas_call(
        attn_kernel,
        out_shape=[heads] * 4
        + [
            jax.ShapeDtypeStruct((width, 3 * local), BF),
            jax.ShapeDtypeStruct((local, width), BF),
        ],
        in_specs=[pl.BlockSpec(memory_space=pltpu.SMEM)] + [vmem] * 4,
        out_specs=[vmem] * 6,
        compiler_params=pltpu.CompilerParams(vmem_limit_bytes=40 * 2**20),
    )(lengths, rounded, qkv_blocks, proj_blocks, qv_bias[0])
    normed_one, inverse_one, middle, middle_rows = run(
        functools.partial(attn_out_kernel, n),
        1,
        [(own, F32), ((own_rows, 1), F32), (own, F32), spread],
        reduce_scratch(n, own_rows, width) + chain_sems(n),
        2 * total_rows * local * width,
        context,
        proj_full,
        inputs,
        branch_bias[0, 0:1],
        norm_gain[0, 0:1],
        norm_bias[0, 0:1],
    )
    middle_rows = middle_rows.reshape(total_rows, width)
    pre_act = jnp.dot(middle_rows, up_full, preferred_element_type=F32) + up_bias[0]
    active = gelu_value(pre_act).astype(BF)
    hidden, dres_two, sums_two, dres_two_all = run(
        functools.partial(turn_kernel, n),
        2,
        [(own, F32), (own, F32), sums, spread],
        reduce_scratch(n, own_rows, width) + chain_sems(n),
        2 * total_rows * width * active.shape[1],
        active,
        down_full,
        middle,
        branch_bias[0, 1:2],
        norm_gain[0, 1:2],
        norm_bias[0, 1:2],
        cotangent,
    )
    dres_two_all = dres_two_all.reshape(total_rows, width)
    dpre = jnp.einsum(
        "rd,fd->rf", dres_two_all, down_full, preferred_element_type=F32
    ) * gelu_slope(pre_act)
    upbias_part = jnp.sum(dpre, axis=0)
    dpre_b = dpre.astype(BF)
    down_part = jnp.einsum("rd,rf->df", dres_two_all, active, preferred_element_type=F32)
    up_part = jnp.einsum("rd,rf->df", middle_rows, dpre_b, preferred_element_type=F32)
    units = active.shape[1]
    shard = width // dp
    dres_one, sums_one, dres_one_all, up_out, down_turned = run(
        functools.partial(mid_back_kernel, n, dp),
        3,
        [(own, F32), sums, spread, ((shard, units), F32), ((shard, units), F32)],
        reduce_scratch(n, own_rows, width)
        + chain_sems(n)
        + [pltpu.VMEM((dp, shard, units), BF)] * 2
        + [pltpu.SemaphoreType.DMA((2, dp))] * 2,
        2 * total_rows * width * dpre_b.shape[1],
        dpre_b,
        up_full,
        dres_two,
        normed_one,
        inverse_one,
        norm_gain[0, 0:1],
        up_part.astype(BF).reshape(dp, shard, units),
        down_part.astype(BF).reshape(dp, shard, units),
    )
    dres_one_all = dres_one_all.reshape(total_rows, width)
    dmixed, qkv_part, proj_part, mix_sums = pl.pallas_call(
        attn_back_kernel,
        out_shape=[
            jax.ShapeDtypeStruct((total_rows, 3 * local), BF),
            jax.ShapeDtypeStruct((width, 3 * local), BF),
            jax.ShapeDtypeStruct((width, local), BF),
            jax.ShapeDtypeStruct((1, 3 * local), F32),
        ],
        in_specs=[pl.BlockSpec(memory_space=pltpu.SMEM)] + [vmem] * 7,
        out_specs=[vmem] * 4,
        scratch_shapes=[pltpu.VMEM((total_rows, local), BF)],
        compiler_params=pltpu.CompilerParams(vmem_limit_bytes=40 * 2**20),
    )(
        lengths, dres_one_all, proj_full, context, rounded, queries_2d, key_2d, values_2d
    )
    all_sums = jnp.concatenate([sums_one, sums_two], axis=0)
    biases = jnp.concatenate([mix_sums, upbias_part.reshape(1, -1)], axis=1)
    upstream, qkv_turned, proj_turned, all_sums, biases = run(
        functools.partial(last_kernel, n, dp),
        4,
        [
            (own, F32),
            ((shard, 3 * local), F32),
            ((shard, local), F32),
            (all_sums.shape, F32),
            (biases.shape, F32),
        ],
        reduce_scratch(n, own_rows, width)
        + [pltpu.VMEM((dp, shard, 3 * local), BF), pltpu.VMEM((dp, shard, local), BF)]
        + [pltpu.SemaphoreType.DMA((4, dp))] * 2
        + [
            pltpu.VMEM((dp,) + all_sums.shape, F32),
            pltpu.VMEM((dp,) + biases.shape, F32),
            pltpu.VMEM((n,) + all_sums.shape, F32),
        ]
        + [pltpu.SemaphoreType.DMA((1, n))] * 2,
        6 * total_rows * local * width,
        dmixed,
        qkv_full,
        dres_one,
        qkv_part.reshape(dp, shard, 3 * local),
        proj_part.reshape(dp, shard, local),
        all_sums,
        biases,
    )
    qkv_out = qkv_turned.reshape(shard, 3, local).transpose(1, 0, 2)
    proj_out = proj_turned.T
    down_out = down_turned.T
    qvbias_out = jnp.stack([biases[0, :local], biases[0, 2 * local : 3 * local]])
    upbias_out = biases[0, 3 * local :]
    pairs = all_sums.reshape(2, 3, width)
    gain_out, normbias_out, branch_out = pairs[:, 0], pairs[:, 1], pairs[:, 2]
    return (
        hidden,
        upstream,
        qkv_out[None],
        qvbias_out[None],
        proj_out[None],
        branch_out[None],
        up_out[None],
        upbias_out[None],
        down_out[None],
        gain_out[None],
        normbias_out[None],
    )


def solution(mesh):
    placed = (
        P(("dp", "tensor"), None),
        P("dp"),
        P(None, None, "dp", "tensor"),
        P(None, None, "tensor"),
        P(None, "tensor", "dp"),
        P(),
        P(None, "dp", "tensor"),
        P(None, "tensor"),
        P(None, "tensor", "dp"),
        P(),
        P(),
        P(("dp", "tensor"), None),
    )
    return jax.shard_map(
        per_device,
        mesh=mesh,
        in_specs=placed,
        out_specs=(
            P(("dp", "tensor"), None),
            P(("dp", "tensor"), None),
            P(None, None, "dp", "tensor"),
            P(None, None, "tensor"),
            P(None, "tensor", "dp"),
            P(),
            P(None, "dp", "tensor"),
            P(None, "tensor"),
            P(None, "tensor", "dp"),
            P(),
            P(),
        ),
        check_vma=False,
    )
```
